512 devices in a mesh: band: 8 (over y, core), pw: 64 (over z, x).
Axes of the slice: x: 4, y: 4, z: 16, core: 2. Of those that a mesh axis runs over, the one named last changes fastest.
Arguments:
- occupied_bands: float32 [2, 16, 3328, 128], P(None, 'band', 'pw'), may hold values from -0.11742834 to 0.11742834
- iterate: float32 [2, 16, 3328, 128], P(None, 'band', 'pw'), may hold values from -2 to 2
- residual: float32 [2, 16, 3328, 128], P(None, 'band', 'pw'), may hold values from -25 to 25, as said below
- old_direction: float32 [2, 16, 3328, 128], P(None, 'band', 'pw'), may hold values from -25 to 25, as said below
- preconditioner: float32 [16, 3328, 128], P('band', 'pw'), may hold values from 0.1 to 1
- old_norm: float32 [16], P('band'), may hold values from 0.4 to 1.6
- eigenvalues: float32 [16], replicated, may hold values from -2 to -0.3
- band_slot: int32 [16], replicated, may hold values from 0 to 15, each once
- potential: float32 [128, 128, 128], P('pw'), may hold values from 0.2 to 1.5
- column_map: int32 [3328], replicated, may hold values from 0 to 16383, as said below
Outputs:
- new_iterate: float32 [2, 16, 3328, 128], P(None, 'band', 'pw')
- new_residual: float32 [2, 16, 3328, 128], P(None, 'band', 'pw')
- direction: float32 [2, 16, 3328, 128], P(None, 'band', 'pw')
- new_norm: float32 [16], P('band')
- density: float32 [128, 128, 128], P('pw', 'band')
The draws below stay inside these ranges and needn't reach their ends.
Inputs may be any that keep to these rules, and one draw needn't show every extreme that they name: `residual`: random draw per entry, rough from column to column and frequency to frequency. `old_direction`: random draw per entry, rough from column to column and frequency to frequency. `column_map`: distinct flat indices; every column with signed a^2 + b^2 < 32^2 is present, the remaining columns lie outside that disc; the column of flat index 0 is present. `band_slot`: each global band index appears once.
All inputs are finite; a program needn't handle non-finite values.
Results may differ from the reference program's by a relative error of at most 0.0001.
Values sent between devices are 32-bit elements; how exact they have to be, the bound alone decides.
A program may use at most 64 MiB of HBM per device.

```python
import math
import jax
import jax.numpy as jnp
from jax import lax

NG = 128
NCOL = 3328
BANDS = 16


def wave_draw(key, salt):
    key = jax.random.fold_in(key, salt)
    subkeys = jax.random.split(key, 3)
    full_shape = (2, BANDS, NCOL, NG)
    position = jnp.arange(NCOL, dtype=jnp.float32) / NCOL
    column_factor = jnp.exp(jax.random.uniform(subkeys[1], (NCOL,), jnp.float32) * math.log(3.2))
    depth_factor = jnp.exp(jax.random.uniform(subkeys[2], (NG,), jnp.float32) * math.log(3.2))
    base_rate = 3.0
    noise_part = jax.random.truncated_normal(subkeys[0], -6.0, 6.0, full_shape, jnp.float32)
    rise_part = jnp.exp(position * math.log(base_rate))
    mean_square = (base_rate * base_rate - 1.0) / (2.0 * math.log(base_rate)) * ((3.2 * 3.2 - 1.0) / (2.0 * math.log(3.2))) ** 2
    scale_part = rise_part * column_factor
    return noise_part * scale_part[None, None, :, None] * depth_factor[None, None, None, :] / math.sqrt(mean_square)


def draw_residual(key, part):
    return wave_draw(key, 11)


def draw_old_direction(key, part):
    return wave_draw(key, 23)


def draw_column_map(key, part):
    key = jax.random.fold_in(key, 37)
    pair_ids = jnp.arange(NG * NG, dtype=jnp.int32)
    wave_x = pair_ids // NG
    wave_y = pair_ids % NG
    wave_x = jnp.where(wave_x < NG // 2, wave_x, wave_x - NG)
    wave_y = jnp.where(wave_y < NG // 2, wave_y, wave_y - NG)
    radius = NG // 4
    outside = (wave_x * wave_x + wave_y * wave_y >= radius * radius).astype(jnp.int32)
    scores = (jax.random.randint(key, (NG * NG,), 0, 4096, dtype=jnp.int32) + outside * 4096) * (NG * NG) + pair_ids
    forced = (pair_ids == 0) | (pair_ids == NG * NG - 1)
    scores = jnp.where(forced, pair_ids - NG * NG, scores)
    ordering = jnp.argsort(scores)
    return ordering[:NCOL].astype(jnp.int32)


def steps_of(stream_key, dims, cuts, smallest, high):
    loudness = 1.0
    for axis_at, blocks in cuts:
        heights = jax.random.uniform(jax.random.fold_in(jax.random.fold_in(stream_key, 6), axis_at), (blocks,), jnp.float32, smallest / len(cuts), high / len(cuts))
        loudness = loudness * jnp.repeat(jnp.exp(heights), dims[axis_at] // blocks).reshape((-1,) + (1,) * (len(dims) - 1 - axis_at))
    return loudness


def centred(rng, dims, deviation, limit, cuts=(), kind=jnp.bfloat16):
    gain = steps_of(rng, dims, cuts, -0.22, 0.18) if cuts else 1.0
    values = jax.random.normal(rng, dims, jnp.float32) * deviation * gain
    return jnp.minimum(jnp.maximum(values, -limit), limit).astype(kind)


def setup_inputs(seed: int = 0) -> dict:
    streams_of = jax.random.split(jax.random.key(seed), 11)
    return {
        "occupied_bands": centred(streams_of[0], (2, BANDS, NCOL, NG), (1.0 / (BANDS * NCOL * NG) ** 0.25), 0.11742834, ((1, 8), (2, 64)), jnp.float32),
        "iterate": centred(streams_of[1], (2, BANDS, NCOL, NG), 0.3, 2.0, ((1, 8), (2, 64)), jnp.float32),
        "residual": draw_residual(jax.random.fold_in(streams_of[10], 71), 0),
        "old_direction": draw_old_direction(jax.random.fold_in(streams_of[10], 71), 0),
        "preconditioner": jnp.clip(jnp.exp(math.log(1.0) - 2.3025851 * jax.random.uniform(streams_of[4], (BANDS, NCOL, NG), jnp.float32) ** steps_of(streams_of[4], (BANDS, NCOL, NG), ((0, 8), (1, 64)), -0.2, 0.2)), 0.1, 1.0),
        "old_norm": jnp.clip(jnp.exp(math.log(1.6) - 1.3862944 * jax.random.uniform(streams_of[5], (BANDS,), jnp.float32) ** steps_of(streams_of[5], (BANDS,), ((0, 8),), -0.2, 0.2)), 0.4, 1.6),
        "eigenvalues": jnp.clip(jax.random.uniform(streams_of[6], (BANDS,), jnp.float32, -2.0, -0.3), -2.0, -0.3),
        "band_slot": jax.random.permutation(streams_of[7], BANDS).astype(jnp.int32),
        "potential": jnp.clip(0.2 + 1.3 * jax.random.uniform(streams_of[8], (NG, NG, NG), jnp.float32) ** steps_of(streams_of[8], (NG, NG, NG), ((0, 64),), -0.2, 0.2), 0.2, 1.5),
        "column_map": draw_column_map(jax.random.fold_in(streams_of[10], 71), 0),
    }


exact_mode = lax.Precision.HIGHEST


def signed_index(values, grid_len):
    return jnp.where(values < grid_len // 2, values, values - grid_len).astype(jnp.int32)


def wave_squares(columns, grid_len):
    wave_x = signed_index(columns // grid_len, grid_len)
    wave_y = signed_index(columns % grid_len, grid_len)
    wave_z = signed_index(jnp.arange(grid_len, dtype=jnp.int32), grid_len)
    return (wave_x * wave_x + wave_y * wave_y)[:, None] + (wave_z * wave_z)[None, :]


def band_lookup(band_slot, eigenvalues):
    select = (band_slot[:, None] == jnp.arange(band_slot.shape[0], dtype=jnp.int32)[None, :]).astype(jnp.float32)
    return jnp.dot(select, eigenvalues, precision=exact_mode)


def to_space(real_part, imag_part, column_map):
    grid_len = real_part.shape[1]
    coefficients = real_part + 1j * imag_part
    full_grid = jnp.zeros((grid_len * grid_len, grid_len), coefficients.dtype).at[column_map].set(coefficients)
    return jnp.fft.ifftn(full_grid.reshape(grid_len, grid_len, grid_len), norm="forward")


def from_space(field_grid, column_map):
    grid_len = field_grid.shape[0]
    coefficients = jnp.fft.fftn(field_grid, norm="forward").reshape(grid_len * grid_len, grid_len)[column_map]
    return jnp.real(coefficients), jnp.imag(coefficients)


def reference(occupied_bands, iterate, residual, old_direction, preconditioner, old_norm, eigenvalues, band_slot, potential, column_map):
    grid_len = potential.shape[0]
    total_pw = column_map.shape[0] * grid_len
    squares = wave_squares(column_map, grid_len)
    kinetic = squares.astype(jnp.float32) * (4.0 / (grid_len * grid_len))
    sphere = (squares < (grid_len // 4) * (grid_len // 4)).astype(jnp.float32)
    occupied = occupied_bands * sphere[None, None]
    start_wave = iterate * sphere[None, None]
    masked_residual = residual * sphere[None, None]
    previous = old_direction * sphere[None, None]
    weight = preconditioner * sphere[None]
    band_energy = band_lookup(band_slot, eigenvalues)
    smoothed = weight[None] * masked_residual
    new_norm = jnp.sum(weight[None] * masked_residual * masked_residual, axis=(0, 2, 3)) / total_pw
    beta_ratio = new_norm / old_norm
    direction = smoothed + beta_ratio[None, :, None, None] * previous
    real_over = jnp.einsum("pvck,pnck->vn", occupied, direction, precision=exact_mode)
    imag_over = jnp.einsum("vck,nck->vn", occupied[0], direction[1], precision=exact_mode) - jnp.einsum("vck,nck->vn", occupied[1], direction[0], precision=exact_mode)
    projected_re = jnp.einsum("vck,vn->nck", occupied[0], real_over, precision=exact_mode) - jnp.einsum("vck,vn->nck", occupied[1], imag_over, precision=exact_mode)
    projected_im = jnp.einsum("vck,vn->nck", occupied[0], imag_over, precision=exact_mode) + jnp.einsum("vck,vn->nck", occupied[1], real_over, precision=exact_mode)
    field_potential = jnp.transpose(potential, (1, 2, 0))

    def apply_one(pair_item):
        field_grid = to_space(pair_item[0], pair_item[1], column_map)
        return from_space(field_grid * field_potential, column_map)

    local_re, local_im = lax.map(apply_one, (direction[0], direction[1]))
    applied = jnp.stack([local_re, local_im]) * sphere[None, None] + (kinetic[None, None] - band_energy[None, :, None, None]) * direction + jnp.stack([projected_re, projected_im])
    curvature = jnp.sum(direction * applied, axis=(0, 2, 3)) / total_pw
    step_size = new_norm / curvature
    new_iterate = start_wave + step_size[None, :, None, None] * direction
    new_residual = masked_residual - step_size[None, :, None, None] * applied

    def add_band(running, items):
        wave_grid = to_space(items[0], items[1], column_map)
        change = to_space(items[2], items[3], column_map)
        return running + jnp.real(jnp.conj(wave_grid) * change), None

    running, unused = lax.scan(add_band, jnp.zeros((grid_len, grid_len, grid_len), jnp.float32), (occupied[0], occupied[1], new_iterate[0], new_iterate[1]))
    density = jnp.transpose(running, (2, 0, 1)) * (4.0 / total_pw)
    return (new_iterate, new_residual, direction, new_norm, density)
```

```python
import math

import jax
import jax.numpy as jnp
import numpy as np
from jax import lax
from jax.sharding import PartitionSpec as P

mode = lax.Precision.HIGH


def rotation(out_index, in_index, grid_len, sign):
    angles = (np.outer(out_index, in_index) % grid_len) * (2.0 * math.pi / grid_len)
    cosine = np.cos(angles)
    sine = np.sin(angles) * sign
    table = np.stack([np.stack([cosine, -sine]), np.stack([sine, cosine])])
    return jnp.asarray(table.astype(np.float32))


def signed_index(values, grid_len):
    return jnp.where(values < grid_len // 2, values, values - grid_len)


def wave_squares(columns, grid_len):
    wave_x = signed_index(columns // grid_len, grid_len)
    wave_y = signed_index(columns % grid_len, grid_len)
    wave_z = signed_index(jnp.arange(grid_len, dtype=jnp.int32), grid_len)
    return (wave_x * wave_x + wave_y * wave_y)[:, None] + (wave_z * wave_z)[None, :]


def halves(values):
    high = lax.reduce_precision(values, 8, 7)
    return high.astype(jnp.bfloat16), (values - high).astype(jnp.bfloat16)


def on_device(
    occupied_bands,
    iterate,
    residual,
    old_direction,
    preconditioner,
    old_norm,
    eigenvalues,
    band_slot,
    potential,
    column_map,
):
    f32 = jnp.float32
    grid_len = potential.shape[1]
    planes = potential.shape[0]
    owners = grid_len // planes
    nb = iterate.shape[1]
    cols = iterate.shape[2]
    slots = band_slot.shape[0]
    groups = slots // nb
    total_pw = column_map.shape[0] * grid_len
    box = grid_len // 2
    wide = -(-(cols + 1) // 8) * 8
    while planes * 2 * nb * (wide - cols) < nb + 2 * slots * nb:
        wide += 8
    spare = wide - cols
    full = np.arange(grid_len)
    inner = np.arange(box) - box // 2
    z_forward = rotation(full, full, grid_len, 1.0)
    z_inverse = rotation(full, full, grid_len, -1.0)
    out_table = rotation(full, inner, grid_len, 1.0)
    in_table = rotation(inner, full, grid_len, -1.0)

    by_owner = column_map.reshape(owners, cols)
    wave_x = signed_index(by_owner // grid_len, grid_len) + box // 2
    wave_y = signed_index(by_owner % grid_len, grid_len) + box // 2
    inside = (wave_x >= 0) & (wave_x < box) & (wave_y >= 0) & (wave_y < box)
    cell = jnp.where(inside, wave_x * box + wave_y, -1)
    cell = jnp.pad(cell, ((0, 0), (0, spare)), constant_values=-1).reshape(-1)
    low_count = min(256, box * box)
    high_count = box * box // low_count
    low_hot = (
        jnp.where(cell < 0, -1, cell % low_count)[:, None]
        == jnp.arange(low_count, dtype=jnp.int32)[None, :]
    ).astype(jnp.bfloat16)
    high_hot = (
        jnp.where(cell < 0, -1, cell // low_count)[None, :]
        == jnp.arange(high_count, dtype=jnp.int32)[:, None]
    )

    my_columns = lax.dynamic_slice_in_dim(column_map, lax.axis_index("pw") * cols, cols)
    squares = wave_squares(my_columns, grid_len)
    kinetic = squares.astype(f32) * (4.0 / (grid_len * grid_len))
    sphere = (squares < grid_len // 4 * (grid_len // 4)).astype(f32)
    occupied = occupied_bands * sphere
    start_wave = iterate * sphere
    masked_residual = residual * sphere
    previous = old_direction * sphere
    weight = preconditioner * sphere
    owner_ids = lax.dynamic_slice_in_dim(band_slot, lax.axis_index("band") * nb, nb)
    band_energy = jnp.sum(
        jnp.where(
            owner_ids[:, None] == jnp.arange(slots, dtype=jnp.int32)[None, :],
            eigenvalues[None, :],
            0.0,
        ),
        axis=1,
    )
    smoothed = weight[None] * masked_residual
    norm_local = jnp.sum(smoothed * masked_residual, axis=(0, 2, 3))

    rows = 2 * nb * cols
    copies = jnp.broadcast_to(occupied.reshape(1, rows, grid_len), (groups, rows, grid_len))
    all_occupied = lax.all_to_all(copies, "band", split_axis=0, concat_axis=0, tiled=True)
    all_occupied = all_occupied.reshape(groups, 2, nb, cols, grid_len)

    stacked = jnp.stack([occupied, start_wave, smoothed, previous], axis=1)
    stacked = jnp.pad(stacked, ((0, 0), (0, 0), (0, 0), (0, spare), (0, 0)))
    mixed = jnp.einsum("rqzk,qfnck->zrfnc", z_forward, stacked, precision=mode)
    mixed = mixed.reshape(owners, planes * 2 * 4, nb * wide)
    lane = jnp.pad(norm_local[:, None], ((0, 0), (cols, spare - 1))).reshape(-1)
    first_row = (jnp.arange(planes * 2 * 4) == 0).astype(f32)
    mixed = mixed + (first_row[:, None] * lane[None, :])[None]
    arrived = lax.all_to_all(mixed, "pw", split_axis=0, concat_axis=0, tiled=True)
    norms = jnp.sum(arrived[:, 0, :], axis=0).reshape(nb, wide)[:, cols]
    new_norm = norms / total_pw
    beta_ratio = new_norm / old_norm

    direction = smoothed + beta_ratio[None, :, None, None] * previous

    arrived = arrived.reshape(owners, planes, 2, 4, nb, wide)
    arrived = arrived.transpose(3, 2, 1, 4, 0, 5).reshape(4, 2 * planes, nb, owners * wide)
    moved = arrived[2] + beta_ratio[None, :, None] * arrived[3]
    fields = jnp.concatenate([arrived[:2], moved[None]], axis=0)
    fields = fields.reshape(3 * 2 * planes * nb, 1, owners * wide)
    high_part, low_part = halves(fields)
    zero = jnp.zeros((), jnp.bfloat16)
    spread = jnp.stack(
        [
            jnp.where(high_hot[None], high_part, zero),
            jnp.where(high_hot[None], low_part, zero),
        ]
    )
    placed = jnp.einsum("hrgc,cl->hrgl", spread, low_hot, preferred_element_type=f32)
    placed = (placed[0] + placed[1]).reshape(3, 2, planes, nb, box, box)
    grid = jnp.einsum("fqpnab,rqyb->frpnay", placed, out_table, precision=mode)
    grid = jnp.einsum("fqpnay,rqxa->frpnxy", grid, out_table, precision=mode)

    occupied_grid = grid[0]
    start_grid = grid[1]
    direction_grid = grid[2]
    started = jnp.sum(occupied_grid * start_grid, axis=(0, 2))
    changed = jnp.sum(occupied_grid * direction_grid, axis=0)
    weighted = potential[None, :, None] * direction_grid
    volume = float(grid_len**3)
    curvature_local = jnp.sum(weighted * direction_grid, axis=(0, 1, 3, 4)) / volume + jnp.sum(
        (kinetic[None, None] - band_energy[None, :, None, None]) * direction * direction,
        axis=(0, 2, 3),
    )
    over_re = jnp.einsum("gqvck,qnck->gvn", all_occupied, direction, precision=mode)
    over_im = jnp.einsum(
        "gvck,nck->gvn", all_occupied[:, 0], direction[1], precision=mode
    ) - jnp.einsum("gvck,nck->gvn", all_occupied[:, 1], direction[0], precision=mode)

    folded = jnp.einsum("qpnxy,rqax->rpnay", weighted, in_table, precision=mode)
    folded = jnp.einsum("qpnay,rqby->rpnab", folded, in_table, precision=mode)
    folded = folded.reshape(2 * planes * nb, high_count, low_count)
    both = jnp.stack(halves(folded))
    picked = jnp.einsum("hrgl,cl->hrgc", both, low_hot, preferred_element_type=f32)
    picked = picked[0] + picked[1]
    picked = jnp.sum(jnp.where(high_hot[None], picked, 0.0), axis=1)
    picked = picked.reshape(2, planes, nb, owners, wide).transpose(3, 1, 0, 2, 4)
    sums = jnp.concatenate([over_re.reshape(-1), over_im.reshape(-1), curvature_local])
    room = planes * 2 * nb * spare
    sums = jnp.pad(sums, (0, room - sums.shape[0])).reshape(1, planes, 2, nb, spare)
    sums = jnp.broadcast_to(sums, (owners,) + sums.shape[1:])
    outgoing = jnp.concatenate([picked[..., :cols], sums], axis=4)
    outgoing = outgoing.reshape(owners, planes * 2, nb * wide)
    returned = lax.all_to_all(outgoing, "pw", split_axis=0, concat_axis=0, tiled=True)
    returned = returned.reshape(owners, planes, 2, nb, wide)
    totals = jnp.sum(returned[..., cols:], axis=0).reshape(-1)
    pairs = slots * nb
    weights_re = totals[:pairs].reshape(groups, nb, nb)
    weights_im = totals[pairs : 2 * pairs].reshape(groups, nb, nb)
    curvature = (
        totals[2 * pairs : 2 * pairs + nb]
        + jnp.sum(weights_re * weights_re + weights_im * weights_im, axis=(0, 1))
    ) / total_pw
    step_size = new_norm / curvature

    density_local = started + jnp.sum(step_size[None, :, None, None] * changed, axis=1)
    density_local = density_local * (4.0 / total_pw)
    strip = grid_len // groups
    density_local = density_local.reshape(planes, groups, strip, grid_len).transpose(1, 0, 2, 3)
    density_local = density_local.reshape(groups, planes * strip, grid_len)
    density = lax.all_to_all(density_local, "band", split_axis=0, concat_axis=0, tiled=True)
    density = jnp.sum(density, axis=0).reshape(planes, strip, grid_len)

    returned = returned.reshape(grid_len, 2, nb, wide)
    local_potential = (
        jnp.einsum("zqnc,rqkz->rnck", returned, z_inverse, precision=mode)[:, :, :cols] / volume
    )
    projected_re = jnp.einsum(
        "gvck,gvn->nck", all_occupied[:, 0], weights_re, precision=mode
    ) - jnp.einsum("gvck,gvn->nck", all_occupied[:, 1], weights_im, precision=mode)
    projected_im = jnp.einsum(
        "gvck,gvn->nck", all_occupied[:, 0], weights_im, precision=mode
    ) + jnp.einsum("gvck,gvn->nck", all_occupied[:, 1], weights_re, precision=mode)
    image = (
        local_potential * sphere
        + (kinetic[None, None] - band_energy[None, :, None, None]) * direction
        + jnp.stack([projected_re, projected_im])
    )
    new_iterate = start_wave + step_size[None, :, None, None] * direction
    new_residual = masked_residual - step_size[None, :, None, None] * image
    return (new_iterate, new_residual, direction, new_norm, density)


def solution(mesh):
    in_specs = (
        P(None, "band", "pw", None),
        P(None, "band", "pw", None),
        P(None, "band", "pw", None),
        P(None, "band", "pw", None),
        P("band", "pw", None),
        P("band"),
        P(),
        P(),
        P("pw", None, None),
        P(),
    )
    out_specs = (
        P(None, "band", "pw", None),
        P(None, "band", "pw", None),
        P(None, "band", "pw", None),
        P("band"),
        P("pw", "band", None),
    )
    return jax.shard_map(
        on_device, mesh=mesh, in_specs=in_specs, out_specs=out_specs, check_vma=False
    )
```

```python
import functools
import math

import jax
import jax.numpy as jnp
import numpy as np
from jax import lax
from jax.experimental import pallas as pl
from jax.experimental.pallas import tpu as pltpu
from jax.sharding import PartitionSpec as P

mode = lax.Precision.HIGH


def rotation(out_index, in_index, grid_len, sign):
    angles = (np.outer(out_index, in_index) % grid_len) * (2.0 * math.pi / grid_len)
    cosine = np.cos(angles)
    sine = np.sin(angles) * sign
    table = np.stack([np.stack([cosine, -sine]), np.stack([sine, cosine])])
    return jnp.asarray(table.astype(np.float32))


def signed_index(values, grid_len):
    return jnp.where(values < grid_len // 2, values, values - grid_len)


def wave_squares(columns, grid_len):
    wave_x = signed_index(columns // grid_len, grid_len)
    wave_y = signed_index(columns % grid_len, grid_len)
    wave_z = signed_index(jnp.arange(grid_len, dtype=jnp.int32), grid_len)
    return (wave_x * wave_x + wave_y * wave_y)[:, None] + (wave_z * wave_z)[None, :]


def halves(values):
    high = lax.reduce_precision(values, 8, 7)
    return high.astype(jnp.bfloat16), (values - high).astype(jnp.bfloat16)


def exchange_kernel(plan, *refs):
    count = len(plan)
    sources, targets = refs[:count], refs[count : 2 * count]
    sems = refs[2 * count :]
    barrier = pltpu.get_barrier_semaphore()
    mesh_ids = pl.DeviceIdType.MESH
    greeted = {}
    for axis, size, _ in plan:
        greeted[axis] = size
    for axis, size in greeted.items():
        me = lax.axis_index(axis)

        @pl.loop(1, size)
        def _(step, axis=axis, size=size, me=me):
            pl.semaphore_signal(
                barrier,
                inc=1,
                device_id={axis: lax.rem(me + step, size)},
                device_id_type=mesh_ids,
            )

    pl.semaphore_wait(barrier, sum(size - 1 for size in greeted.values()))

    def copy_of(which, step):
        axis, size, whole = plan[which]
        me = lax.axis_index(axis)
        peer = lax.rem(me + step, size)
        send_sem, recv_sem = sems[2 * which], sems[2 * which + 1]
        return pltpu.make_async_remote_copy(
            src_ref=sources[which] if whole else sources[which].at[peer],
            dst_ref=targets[which].at[me],
            send_sem=send_sem.at[step],
            recv_sem=recv_sem.at[step],
            device_id={axis: peer},
            device_id_type=mesh_ids,
        )

    for which, (axis, size, whole) in enumerate(plan):
        half = size // 2
        copy_of(which, half).start()

        @pl.loop(1, half)
        def _(near, which=which, half=half, size=size):
            copy_of(which, half - near).start()
            copy_of(which, half + near).start()

    for which, (axis, size, whole) in enumerate(plan):
        me = lax.axis_index(axis)
        if whole:
            targets[which][me] = sources[which][...]
        else:
            targets[which][me] = sources[which][me]
    for which, (axis, size, whole) in enumerate(plan):

        @pl.loop(1, size)
        def _(step, which=which):
            copy_of(which, step).wait()


def exchange(collective_id, plan, *arrays):
    shapes, scratch = [], []
    for (axis, size, whole), array in zip(plan, arrays):
        shape = ((size,) + array.shape) if whole else array.shape
        shapes.append(jax.ShapeDtypeStruct(shape, array.dtype))
        scratch += [pltpu.SemaphoreType.DMA((size,)), pltpu.SemaphoreType.DMA((size,))]
    return pl.pallas_call(
        functools.partial(exchange_kernel, plan),
        out_shape=shapes,
        in_specs=[pl.BlockSpec(memory_space=pltpu.VMEM)] * len(arrays),
        out_specs=[pl.BlockSpec(memory_space=pltpu.VMEM)] * len(arrays),
        scratch_shapes=scratch,
        compiler_params=pltpu.CompilerParams(
            collective_id=collective_id, has_side_effects=True
        ),
    )(*arrays)


def on_device(
    occupied_bands,
    iterate,
    residual,
    old_direction,
    preconditioner,
    old_norm,
    eigenvalues,
    band_slot,
    potential,
    column_map,
):
    f32 = jnp.float32
    grid_len = potential.shape[1]
    planes = potential.shape[0]
    owners = grid_len // planes
    nb = iterate.shape[1]
    cols = iterate.shape[2]
    slots = band_slot.shape[0]
    groups = slots // nb
    total_pw = column_map.shape[0] * grid_len
    box = grid_len // 2
    wide = -(-(cols + 1) // 8) * 8
    while planes * 2 * nb * (wide - cols) < nb + 2 * slots * nb:
        wide += 8
    spare = wide - cols
    full = np.arange(grid_len)
    inner = np.arange(box) - box // 2
    z_forward = rotation(full, full, grid_len, 1.0)
    z_inverse = rotation(full, full, grid_len, -1.0)
    out_table = rotation(full, inner, grid_len, 1.0)
    in_table = rotation(inner, full, grid_len, -1.0)

    by_owner = column_map.reshape(owners, cols)
    wave_x = signed_index(by_owner // grid_len, grid_len) + box // 2
    wave_y = signed_index(by_owner % grid_len, grid_len) + box // 2
    inside = (wave_x >= 0) & (wave_x < box) & (wave_y >= 0) & (wave_y < box)
    cell = jnp.where(inside, wave_x * box + wave_y, -1)
    cell = jnp.pad(cell, ((0, 0), (0, spare)), constant_values=-1).reshape(-1)
    low_count = min(256, box * box)
    high_count = box * box // low_count
    low_hot = (
        jnp.where(cell < 0, -1, cell % low_count)[:, None]
        == jnp.arange(low_count, dtype=jnp.int32)[None, :]
    ).astype(jnp.bfloat16)
    high_hot = (
        jnp.where(cell < 0, -1, cell // low_count)[None, :]
        == jnp.arange(high_count, dtype=jnp.int32)[:, None]
    )

    my_columns = lax.dynamic_slice_in_dim(column_map, lax.axis_index("pw") * cols, cols)
    squares = wave_squares(my_columns, grid_len)
    kinetic = squares.astype(f32) * (4.0 / (grid_len * grid_len))
    sphere = (squares < grid_len // 4 * (grid_len // 4)).astype(f32)
    occupied = occupied_bands * sphere
    start_wave = iterate * sphere
    masked_residual = residual * sphere
    previous = old_direction * sphere
    weight = preconditioner * sphere
    owner_ids = lax.dynamic_slice_in_dim(band_slot, lax.axis_index("band") * nb, nb)
    band_energy = jnp.sum(
        jnp.where(
            owner_ids[:, None] == jnp.arange(slots, dtype=jnp.int32)[None, :],
            eigenvalues[None, :],
            0.0,
        ),
        axis=1,
    )
    smoothed = weight[None] * masked_residual
    norm_local = jnp.sum(smoothed * masked_residual, axis=(0, 2, 3))

    stacked = jnp.stack([occupied, start_wave, smoothed, previous], axis=1)
    stacked = jnp.pad(stacked, ((0, 0), (0, 0), (0, 0), (0, spare), (0, 0)))
    mixed = jnp.einsum("rqzk,qfnck->zrfnc", z_forward, stacked, precision=mode)
    mixed = mixed.reshape(owners, planes * 2 * 4, nb * wide)
    lane = jnp.pad(norm_local[:, None], ((0, 0), (cols, spare - 1))).reshape(-1)
    first_row = (jnp.arange(planes * 2 * 4) == 0).astype(f32)
    mixed = mixed + (first_row[:, None] * lane[None, :])[None]
    arrived, all_occupied = exchange(
        0,
        (("pw", owners, False), ("band", groups, True)),
        mixed,
        occupied.reshape(2 * nb, cols, grid_len),
    )
    all_occupied = all_occupied.reshape(groups, 2, nb, cols, grid_len)
    norms = jnp.sum(arrived[:, 0, :], axis=0).reshape(nb, wide)[:, cols]
    new_norm = norms / total_pw
    beta_ratio = new_norm / old_norm

    direction = smoothed + beta_ratio[None, :, None, None] * previous

    arrived = arrived.reshape(owners, planes, 2, 4, nb, wide)
    arrived = arrived.transpose(3, 2, 1, 4, 0, 5).reshape(4, 2 * planes, nb, owners * wide)
    moved = arrived[2] + beta_ratio[None, :, None] * arrived[3]
    fields = jnp.concatenate([arrived[:2], moved[None]], axis=0)
    fields = fields.reshape(3 * 2 * planes * nb, 1, owners * wide)
    high_part, low_part = halves(fields)
    zero = jnp.zeros((), jnp.bfloat16)
    spread = jnp.stack(
        [
            jnp.where(high_hot[None], high_part, zero),
            jnp.where(high_hot[None], low_part, zero),
        ]
    )
    placed = jnp.einsum("hrgc,cl->hrgl", spread, low_hot, preferred_element_type=f32)
    placed = (placed[0] + placed[1]).reshape(3, 2, planes, nb, box, box)
    grid = jnp.einsum("fqpnab,rqyb->frpnay", placed, out_table, precision=mode)
    grid = jnp.einsum("fqpnay,rqxa->frpnxy", grid, out_table, precision=mode)

    occupied_grid = grid[0]
    start_grid = grid[1]
    direction_grid = grid[2]
    started = jnp.sum(occupied_grid * start_grid, axis=(0, 2))
    changed = jnp.sum(occupied_grid * direction_grid, axis=0)
    weighted = potential[None, :, None] * direction_grid
    volume = float(grid_len**3)
    curvature_local = jnp.sum(weighted * direction_grid, axis=(0, 1, 3, 4)) / volume + jnp.sum(
        (kinetic[None, None] - band_energy[None, :, None, None]) * direction * direction,
        axis=(0, 2, 3),
    )
    over = jnp.einsum("gqvck,rnck->qrgvn", all_occupied, direction, precision=mode)
    over_re = over[0, 0] + over[1, 1]
    over_im = over[0, 1] - over[1, 0]

    folded = jnp.einsum("qpnxy,rqax->rpnay", weighted, in_table, precision=mode)
    folded = jnp.einsum("qpnay,rqby->rpnab", folded, in_table, precision=mode)
    folded = folded.reshape(2 * planes * nb, high_count, low_count)
    both = jnp.stack(halves(folded))
    picked = jnp.einsum("hrgl,cl->hrgc", both, low_hot, preferred_element_type=f32)
    picked = picked[0] + picked[1]
    picked = jnp.sum(jnp.where(high_hot[None], picked, 0.0), axis=1)
    picked = picked.reshape(2, planes, nb, owners, wide).transpose(3, 1, 0, 2, 4)
    sums = jnp.concatenate([over_re.reshape(-1), over_im.reshape(-1), curvature_local])
    room = planes * 2 * nb * spare
    sums = jnp.pad(sums, (0, room - sums.shape[0])).reshape(1, planes, 2, nb, spare)
    sums = jnp.broadcast_to(sums, (owners,) + sums.shape[1:])
    outgoing = jnp.concatenate([picked[..., :cols], sums], axis=4)
    outgoing = outgoing.reshape(owners, planes * 2, nb * wide)
    (returned,) = exchange(1, (("pw", owners, False),), outgoing)
    returned = returned.reshape(owners, planes, 2, nb, wide)
    totals = jnp.sum(returned[..., cols:], axis=0).reshape(-1)
    pairs = slots * nb
    weights_re = totals[:pairs].reshape(groups, nb, nb)
    weights_im = totals[pairs : 2 * pairs].reshape(groups, nb, nb)
    curvature = (
        totals[2 * pairs : 2 * pairs + nb]
        + jnp.sum(weights_re * weights_re + weights_im * weights_im, axis=(0, 1))
    ) / total_pw
    step_size = new_norm / curvature

    density_local = started + jnp.sum(step_size[None, :, None, None] * changed, axis=1)
    density_local = density_local * (4.0 / total_pw)
    strip = grid_len // groups
    density_local = density_local.reshape(planes, groups, strip, grid_len).transpose(1, 0, 2, 3)
    density_local = density_local.reshape(groups, planes * strip, grid_len)
    (density,) = exchange(2, (("band", groups, False),), density_local)
    density = jnp.sum(density, axis=0).reshape(planes, strip, grid_len)

    returned = returned.reshape(grid_len, 2, nb, wide)
    local_potential = (
        jnp.einsum("zqnc,rqkz->rnck", returned, z_inverse, precision=mode)[:, :, :cols] / volume
    )
    mixing = jnp.stack(
        [jnp.stack([weights_re, weights_im]), jnp.stack([-weights_im, weights_re])]
    )
    projected = jnp.einsum("gqvck,qrgvn->rnck", all_occupied, mixing, precision=mode)
    image = (
        local_potential * sphere
        + (kinetic[None, None] - band_energy[None, :, None, None]) * direction
        + projected
    )
    new_iterate = start_wave + step_size[None, :, None, None] * direction
    new_residual = masked_residual - step_size[None, :, None, None] * image
    return (new_iterate, new_residual, direction, new_norm, density)


def solution(mesh):
    in_specs = (
        P(None, "band", "pw", None),
        P(None, "band", "pw", None),
        P(None, "band", "pw", None),
        P(None, "band", "pw", None),
        P("band", "pw", None),
        P("band"),
        P(),
        P(),
        P("pw", None, None),
        P(),
    )
    out_specs = (
        P(None, "band", "pw", None),
        P(None, "band", "pw", None),
        P(None, "band", "pw", None),
        P("band"),
        P("pw", "band", None),
    )
    return jax.shard_map(
        on_device, mesh=mesh, in_specs=in_specs, out_specs=out_specs, check_vma=False
    )
```

```python
import functools
import math

import jax
import jax.numpy as jnp
import numpy as np
from jax import lax
from jax.experimental import pallas as pl
from jax.experimental.pallas import tpu as pltpu
from jax.sharding import PartitionSpec as P

mode = lax.Precision.HIGH


def rotation(out_index, in_index, grid_len, sign):
    angles = (np.outer(out_index, in_index) % grid_len) * (2.0 * math.pi / grid_len)
    cosine = np.cos(angles)
    sine = np.sin(angles) * sign
    table = np.stack([np.stack([cosine, -sine]), np.stack([sine, cosine])])
    return jnp.asarray(table.astype(np.float32))


def signed_index(values, grid_len):
    return jnp.where(values < grid_len // 2, values, values - grid_len)


def wave_squares(columns, grid_len):
    wave_x = signed_index(columns // grid_len, grid_len)
    wave_y = signed_index(columns % grid_len, grid_len)
    wave_z = signed_index(jnp.arange(grid_len, dtype=jnp.int32), grid_len)
    return (wave_x * wave_x + wave_y * wave_y)[:, None] + (wave_z * wave_z)[None, :]


def halves(values):
    high = lax.reduce_precision(values, 8, 7)
    return high.astype(jnp.bfloat16), (values - high).astype(jnp.bfloat16)


def exchange_kernel(plan, *refs):
    count = len(plan)
    sources, targets = refs[:count], refs[count : 2 * count]
    sems = refs[2 * count :]
    barrier = pltpu.get_barrier_semaphore()
    mesh_ids = pl.DeviceIdType.MESH
    greeted = {}
    for axis, size, _ in plan:
        greeted[axis] = size
    for axis, size in greeted.items():
        me = lax.axis_index(axis)

        @pl.loop(1, size)
        def _(step, axis=axis, size=size, me=me):
            pl.semaphore_signal(
                barrier,
                inc=1,
                device_id={axis: lax.rem(me + step, size)},
                device_id_type=mesh_ids,
            )

    pl.semaphore_wait(barrier, sum(size - 1 for size in greeted.values()))

    def copy_of(which, step):
        axis, size, whole = plan[which]
        me = lax.axis_index(axis)
        peer = lax.rem(me + step, size)
        send_sem, recv_sem = sems[2 * which], sems[2 * which + 1]
        return pltpu.make_async_remote_copy(
            src_ref=sources[which] if whole else sources[which].at[peer],
            dst_ref=targets[which].at[me],
            send_sem=send_sem.at[step],
            recv_sem=recv_sem.at[step],
            device_id={axis: peer},
            device_id_type=mesh_ids,
        )

    for which, (axis, size, whole) in enumerate(plan):
        half = size // 2
        copy_of(which, half).start()

        @pl.loop(1, half)
        def _(near, which=which, half=half, size=size):
            copy_of(which, half - near).start()
            copy_of(which, half + near).start()

    for which, (axis, size, whole) in enumerate(plan):
        me = lax.axis_index(axis)
        if whole:
            targets[which][me] = sources[which][...]
        else:
            targets[which][me] = sources[which][me]
    for which, (axis, size, whole) in enumerate(plan):

        @pl.loop(1, size)
        def _(step, which=which):
            copy_of(which, step).wait()


def exchange(collective_id, plan, *arrays):
    shapes, scratch = [], []
    for (axis, size, whole), array in zip(plan, arrays):
        shape = ((size,) + array.shape) if whole else array.shape
        shapes.append(jax.ShapeDtypeStruct(shape, array.dtype))
        scratch += [pltpu.SemaphoreType.DMA((size,)), pltpu.SemaphoreType.DMA((size,))]
    return pl.pallas_call(
        functools.partial(exchange_kernel, plan),
        out_shape=shapes,
        in_specs=[pl.BlockSpec(memory_space=pltpu.VMEM)] * len(arrays),
        out_specs=[pl.BlockSpec(memory_space=pltpu.VMEM)] * len(arrays),
        scratch_shapes=scratch,
        compiler_params=pltpu.CompilerParams(
            collective_id=collective_id, has_side_effects=True
        ),
    )(*arrays)


def greet(axes):
    barrier = pltpu.get_barrier_semaphore()
    for axis, size in axes:
        me = lax.axis_index(axis)

        @pl.loop(1, size)
        def _(step, axis=axis, size=size, me=me):
            pl.semaphore_signal(
                barrier,
                inc=1,
                device_id={axis: lax.rem(me + step, size)},
                device_id_type=pl.DeviceIdType.MESH,
            )

    return barrier, sum(size - 1 for _, size in axes)


def sender(axis, size, source, target, sems):
    me = lax.axis_index(axis)

    def copy_of(step):
        peer = lax.rem(me + step, size)
        return pltpu.make_async_remote_copy(
            src_ref=source(peer),
            dst_ref=target(me),
            send_sem=sems[0].at[step],
            recv_sem=sems[1].at[step],
            device_id={axis: peer},
            device_id_type=pl.DeviceIdType.MESH,
        )

    def start():
        half = size // 2
        copy_of(half).start()

        @pl.loop(1, half)
        def _(near):
            copy_of(half - near).start()
            copy_of(half + near).start()

    def wait():
        @pl.loop(1, size)
        def _(step):
            copy_of(step).wait()

    return start, wait


def finish_kernel(
    sizes,
    outgoing,
    all_occupied,
    direction,
    curvature_row,
    norm_row,
    started,
    changed,
    returned,
    total_row,
    density,
    rows,
    sums,
    all_sums,
    local_density,
    strips,
    *sems,
):
    owners, groups, nb, total_pw = sizes
    pairs = groups * 2 * nb * nb
    me, my_group = lax.axis_index("pw"), lax.axis_index("band")
    barrier, greetings = greet((("pw", owners), ("band", groups)))

    rows[...] = jnp.zeros_like(rows)

    @pl.loop(0, groups)
    def _(group):
        real, imag = [], []
        for there in range(nb):
            occ_re = all_occupied[group, there]
            occ_im = all_occupied[group, nb + there]
            for here in range(nb):
                dir_re, dir_im = direction[here], direction[nb + here]
                real.append(jnp.sum(occ_re * dir_re + occ_im * dir_im, axis=0, keepdims=True))
                imag.append(jnp.sum(occ_re * dir_im - occ_im * dir_re, axis=0, keepdims=True))
        height = 2 * nb * nb
        start = pl.multiple_of(group * height, height)
        rows[pl.ds(start, height), :] = jnp.concatenate(real + imag, axis=0)

    lanes = lax.dot_general(
        jnp.ones((8, rows.shape[1]), jnp.float32),
        rows[...],
        (((1,), (1,)), ((), ())),
        precision=lax.Precision.HIGHEST,
        preferred_element_type=jnp.float32,
    )
    sums[...] = lanes[0:1] + curvature_row[...]
    all_sums[me] = sums[...]
    returned[me] = outgoing[me]
    pl.semaphore_wait(barrier, greetings)

    sums_start, sums_wait = sender(
        "pw", owners, lambda peer: sums, lambda mine: all_sums.at[mine], sems[0:2]
    )
    back_start, back_wait = sender(
        "pw",
        owners,
        lambda peer: outgoing.at[peer],
        lambda mine: returned.at[mine],
        sems[2:4],
    )
    dens_start, dens_wait = sender(
        "band",
        groups,
        lambda peer: local_density.at[peer],
        lambda mine: strips.at[mine],
        sems[4:6],
    )
    sums_start()
    back_start()
    sums_wait()
    totals = jnp.sum(all_sums[...], axis=0)
    total_row[...] = totals
    lane = lax.broadcasted_iota(jnp.int32, totals.shape, 1)
    steps = []
    for band in range(nb):
        squares = jnp.where((lane < pairs) & (lax.rem(lane, nb) == band), totals * totals, 0.0)
        own = jnp.where(lane == pairs + band, totals, 0.0)
        curvature = jnp.sum(squares + own, axis=1, keepdims=True) / total_pw
        norm = jnp.sum(
            jnp.where(lane == band, norm_row[...], 0.0), axis=1, keepdims=True
        )
        steps.append(norm / curvature)
    planes, width = started.shape[0], started.shape[1] // groups
    for group in range(groups):
        for plane in range(planes):
            part = slice(group * width, (group + 1) * width)
            value = started[plane, part, :]
            for band in range(nb):
                value = value + steps[band] * changed[plane, band, part, :]
            local_density[group, plane * width : (plane + 1) * width, :] = value * (
                4.0 / total_pw
            )
    strips[my_group] = local_density[my_group]
    dens_start()
    dens_wait()
    density[...] = jnp.sum(strips[...], axis=0)
    back_wait()


def finish(sizes, outgoing, all_occupied, direction, curvature_row, norm_row, started, changed):
    owners, groups, nb, _ = sizes
    planes, grid_len = started.shape[0], started.shape[1]
    f32 = jnp.float32
    height = planes * grid_len // groups
    vmem = pl.BlockSpec(memory_space=pltpu.VMEM)
    lanes = curvature_row.shape[1]
    sems = []
    for size in (owners, owners, groups):
        sems += [pltpu.SemaphoreType.DMA((size,)), pltpu.SemaphoreType.DMA((size,))]
    return pl.pallas_call(
        functools.partial(finish_kernel, sizes),
        out_shape=[
            jax.ShapeDtypeStruct(outgoing.shape, f32),
            jax.ShapeDtypeStruct((1, lanes), f32),
            jax.ShapeDtypeStruct((height, started.shape[2]), f32),
        ],
        in_specs=[vmem] * 7,
        out_specs=[vmem] * 3,
        scratch_shapes=[
            pltpu.VMEM((lanes, grid_len), f32),
            pltpu.VMEM((1, lanes), f32),
            pltpu.VMEM((owners, 1, lanes), f32),
            pltpu.VMEM((groups, height, started.shape[2]), f32),
            pltpu.VMEM((groups, height, started.shape[2]), f32),
        ]
        + sems,
        compiler_params=pltpu.CompilerParams(collective_id=1, has_side_effects=True),
    )(outgoing, all_occupied, direction, curvature_row, norm_row, started, changed)


def on_device(
    occupied_bands,
    iterate,
    residual,
    old_direction,
    preconditioner,
    old_norm,
    eigenvalues,
    band_slot,
    potential,
    column_map,
):
    f32 = jnp.float32
    grid_len = potential.shape[1]
    planes = potential.shape[0]
    owners = grid_len // planes
    nb = iterate.shape[1]
    cols = iterate.shape[2]
    slots = band_slot.shape[0]
    groups = slots // nb
    total_pw = column_map.shape[0] * grid_len
    box = grid_len // 2
    wide = -(-(cols + 1) // 64) * 64
    spare = wide - cols
    full = np.arange(grid_len)
    inner = np.arange(box) - box // 2
    z_forward = rotation(full, full, grid_len, 1.0)
    z_inverse = rotation(full, full, grid_len, -1.0)
    out_table = rotation(full, inner, grid_len, 1.0)
    in_table = rotation(inner, full, grid_len, -1.0)

    by_owner = column_map.reshape(owners, cols)
    wave_x = signed_index(by_owner // grid_len, grid_len) + box // 2
    wave_y = signed_index(by_owner % grid_len, grid_len) + box // 2
    inside = (wave_x >= 0) & (wave_x < box) & (wave_y >= 0) & (wave_y < box)
    cell = jnp.where(inside, wave_x * box + wave_y, -1)
    cell = jnp.pad(cell, ((0, 0), (0, spare)), constant_values=-1).reshape(-1)
    low_count = min(256, box * box)
    high_count = box * box // low_count
    low_hot = (
        jnp.where(cell < 0, -1, cell % low_count)[:, None]
        == jnp.arange(low_count, dtype=jnp.int32)[None, :]
    ).astype(jnp.bfloat16)
    high_hot = (
        jnp.where(cell < 0, -1, cell // low_count)[None, :]
        == jnp.arange(high_count, dtype=jnp.int32)[:, None]
    )

    my_columns = lax.dynamic_slice_in_dim(column_map, lax.axis_index("pw") * cols, cols)
    squares = wave_squares(my_columns, grid_len)
    kinetic = squares.astype(f32) * (4.0 / (grid_len * grid_len))
    sphere = (squares < grid_len // 4 * (grid_len // 4)).astype(f32)
    occupied = occupied_bands * sphere
    start_wave = iterate * sphere
    masked_residual = residual * sphere
    previous = old_direction * sphere
    weight = preconditioner * sphere
    owner_ids = lax.dynamic_slice_in_dim(band_slot, lax.axis_index("band") * nb, nb)
    band_energy = jnp.sum(
        jnp.where(
            owner_ids[:, None] == jnp.arange(slots, dtype=jnp.int32)[None, :],
            eigenvalues[None, :],
            0.0,
        ),
        axis=1,
    )
    smoothed = weight[None] * masked_residual
    norm_local = jnp.sum(smoothed * masked_residual, axis=(0, 2, 3))

    stacked = jnp.stack([occupied, start_wave, smoothed, previous], axis=1)
    stacked = jnp.pad(stacked, ((0, 0), (0, 0), (0, 0), (0, spare), (0, 0)))
    mixed = jnp.einsum("rqzk,qfnck->zrfnc", z_forward, stacked, precision=mode)
    mixed = mixed.reshape(owners, planes * 2 * 4, nb * wide)
    lane = jnp.pad(norm_local[:, None], ((0, 0), (cols, spare - 1))).reshape(-1)
    first_row = (jnp.arange(planes * 2 * 4) == 0).astype(f32)
    mixed = mixed + (first_row[:, None] * lane[None, :])[None]
    arrived, all_occupied = exchange(
        0,
        (("pw", owners, False), ("band", groups, True)),
        mixed,
        occupied.reshape(2 * nb, cols, grid_len),
    )
    norms = jnp.sum(arrived[:, 0, :], axis=0).reshape(nb, wide)[:, cols]
    new_norm = norms / total_pw
    beta_ratio = new_norm / old_norm

    direction = smoothed + beta_ratio[None, :, None, None] * previous

    arrived = arrived.reshape(owners, planes, 2, 4, nb, wide)
    arrived = arrived.transpose(3, 2, 1, 4, 0, 5).reshape(4, 2 * planes, nb, owners * wide)
    moved = arrived[2] + beta_ratio[None, :, None] * arrived[3]
    fields = jnp.concatenate([arrived[:2], moved[None]], axis=0)
    fields = fields.reshape(3 * 2 * planes * nb, 1, owners * wide)
    high_part, low_part = halves(fields)
    zero = jnp.zeros((), jnp.bfloat16)
    spread = jnp.stack(
        [
            jnp.where(high_hot[None], high_part, zero),
            jnp.where(high_hot[None], low_part, zero),
        ]
    )
    placed = jnp.einsum("hrgc,cl->hrgl", spread, low_hot, preferred_element_type=f32)
    placed = (placed[0] + placed[1]).reshape(3, 2, planes, nb, box, box)
    grid = jnp.einsum("fqpnab,rqyb->frpnay", placed, out_table, precision=mode)
    grid = jnp.einsum("fqpnay,rqxa->frpnxy", grid, out_table, precision=mode)

    occupied_grid = grid[0]
    start_grid = grid[1]
    direction_grid = grid[2]
    started = jnp.sum(occupied_grid * start_grid, axis=(0, 2))
    changed = jnp.sum(occupied_grid * direction_grid, axis=0)
    weighted = potential[None, :, None] * direction_grid
    volume = float(grid_len**3)
    curvature_local = jnp.sum(weighted * direction_grid, axis=(0, 1, 3, 4)) / volume + jnp.sum(
        (kinetic[None, None] - band_energy[None, :, None, None]) * direction * direction,
        axis=(0, 2, 3),
    )

    folded = jnp.einsum("qpnxy,rqax->rpnay", weighted, in_table, precision=mode)
    folded = jnp.einsum("qpnay,rqby->rpnab", folded, in_table, precision=mode)
    folded = folded.reshape(2 * planes * nb, high_count, low_count)
    both = jnp.stack(halves(folded))
    picked = jnp.einsum("hrgl,cl->hrgc", both, low_hot, preferred_element_type=f32)
    picked = picked[0] + picked[1]
    picked = jnp.sum(jnp.where(high_hot[None], picked, 0.0), axis=1)
    picked = picked.reshape(2, planes, nb, owners, wide).transpose(3, 1, 0, 2, 4)
    outgoing = picked.reshape(owners, planes * 2, nb * wide)
    pairs = slots * nb
    lanes = 128
    returned, totals, density = finish(
        (owners, groups, nb, float(total_pw)),
        outgoing,
        all_occupied,
        direction.reshape(2 * nb, cols, grid_len),
        jnp.pad(curvature_local, (2 * pairs, lanes - 2 * pairs - nb)).reshape(1, lanes),
        jnp.pad(new_norm, (0, lanes - nb)).reshape(1, lanes),
        started,
        changed,
    )
    density = density.reshape(planes, grid_len // groups, grid_len)
    totals = totals.reshape(-1)
    found = totals[: 2 * pairs].reshape(groups, 2, nb, nb)
    curvature = (
        totals[2 * pairs : 2 * pairs + nb] + jnp.sum(found * found, axis=(0, 1, 2))
    ) / total_pw
    step_size = new_norm / curvature

    returned = returned.reshape(grid_len, 2, nb, wide)
    local_potential = (
        jnp.einsum("zqnc,rqkz->rnck", returned, z_inverse, precision=mode)[:, :, :cols] / volume
    )
    mixing = jnp.stack([found, jnp.stack([-found[:, 1], found[:, 0]], axis=1)], axis=1)
    all_occupied = all_occupied.reshape(groups, 2, nb, cols, grid_len)
    projected = jnp.einsum("gqvck,gqrvn->rnck", all_occupied, mixing, precision=mode)
    image = (
        local_potential * sphere
        + (kinetic[None, None] - band_energy[None, :, None, None]) * direction
        + projected
    )
    new_iterate = start_wave + step_size[None, :, None, None] * direction
    new_residual = masked_residual - step_size[None, :, None, None] * image
    return (new_iterate, new_residual, direction, new_norm, density)


def solution(mesh):
    in_specs = (
        P(None, "band", "pw", None),
        P(None, "band", "pw", None),
        P(None, "band", "pw", None),
        P(None, "band", "pw", None),
        P("band", "pw", None),
        P("band"),
        P(),
        P(),
        P("pw", None, None),
        P(),
    )
    out_specs = (
        P(None, "band", "pw", None),
        P(None, "band", "pw", None),
        P(None, "band", "pw", None),
        P("band"),
        P("pw", "band", None),
    )
    return jax.shard_map(
        on_device, mesh=mesh, in_specs=in_specs, out_specs=out_specs, check_vma=False
    )
```

```python
import functools
import math

import jax
import jax.numpy as jnp
import numpy as np
from jax import lax
from jax.experimental import pallas as pl
from jax.experimental.pallas import tpu as pltpu
from jax.sharding import PartitionSpec as P

mode = lax.Precision.HIGH


def rotation(out_index, in_index, grid_len, sign):
    angles = (np.outer(out_index, in_index) % grid_len) * (2.0 * math.pi / grid_len)
    cosine = np.cos(angles)
    sine = np.sin(angles) * sign
    table = np.stack([np.stack([cosine, -sine]), np.stack([sine, cosine])])
    return jnp.asarray(table.astype(np.float32))


def signed_index(values, grid_len):
    return jnp.where(values < grid_len // 2, values, values - grid_len)


def wave_squares(columns, grid_len):
    wave_x = signed_index(columns // grid_len, grid_len)
    wave_y = signed_index(columns % grid_len, grid_len)
    wave_z = signed_index(jnp.arange(grid_len, dtype=jnp.int32), grid_len)
    return (wave_x * wave_x + wave_y * wave_y)[:, None] + (wave_z * wave_z)[None, :]


def halves(values):
    high = lax.reduce_precision(values, 8, 7)
    return high.astype(jnp.bfloat16), (values - high).astype(jnp.bfloat16)


def greet(axes):
    barrier = pltpu.get_barrier_semaphore()
    for axis, size in axes:
        me = lax.axis_index(axis)

        @pl.loop(1, size)
        def _(step, axis=axis, size=size, me=me):
            pl.semaphore_signal(
                barrier,
                inc=1,
                device_id={axis: lax.rem(me + step, size)},
                device_id_type=pl.DeviceIdType.MESH,
            )

    return barrier, sum(size - 1 for _, size in axes)


def sender(axis, size, source, target, sems):
    me = lax.axis_index(axis)

    def copy_of(step):
        peer = lax.rem(me + step, size)
        return pltpu.make_async_remote_copy(
            src_ref=source(peer),
            dst_ref=target(me),
            send_sem=sems[0].at[step],
            recv_sem=sems[1].at[step],
            device_id={axis: peer},
            device_id_type=pl.DeviceIdType.MESH,
        )

    def start():
        half = size // 2
        copy_of(half).start()

        @pl.loop(1, half)
        def _(near):
            copy_of(half - near).start()
            copy_of(half + near).start()

    def wait():
        @pl.loop(1, size)
        def _(step):
            copy_of(step).wait()

    return start, wait


def band_value(row, lane, band):
    return jnp.sum(jnp.where(lane == band, row, 0.0), axis=1, keepdims=True)


def begin_kernel(
    sizes,
    stacked,
    table,
    norm_row,
    old_row,
    occupied,
    both_here,
    moved_here,
    all_occupied,
    total_row,
    both,
    moved,
    smooth,
    former,
    all_norms,
    *sems,
):
    owners, groups, nb, total_pw = sizes
    me, my_group = lax.axis_index("pw"), lax.axis_index("band")
    barrier, greetings = greet((("pw", owners), ("band", groups)))
    parts = table.shape[1] // owners

    def mixed(field):
        return sum(
            lax.dot_general(
                table[part],
                stacked[part, field],
                (((1,), (1,)), ((), ())),
                precision=lax.Precision.HIGHEST,
                preferred_element_type=jnp.float32,
            )
            for part in range(2)
        )

    for field in range(2):
        value = mixed(field)
        for part in range(parts):
            both[:, part * 2 + field, :] = value[part * owners : (part + 1) * owners]
    smooth[...] = mixed(2)
    former[...] = mixed(3)
    all_norms[me] = norm_row[...]
    both_here[me] = both[me]
    all_occupied[my_group] = occupied[...]
    pl.semaphore_wait(barrier, greetings)

    norm_start, norm_wait = sender(
        "pw", owners, lambda peer: norm_row, lambda mine: all_norms.at[mine], sems[0:2]
    )
    both_start, both_wait = sender(
        "pw", owners, lambda peer: both.at[peer], lambda mine: both_here.at[mine], sems[2:4]
    )
    move_start, move_wait = sender(
        "pw", owners, lambda peer: moved.at[peer], lambda mine: moved_here.at[mine], sems[4:6]
    )
    occ_start, occ_wait = sender(
        "band", groups, lambda peer: occupied, lambda mine: all_occupied.at[mine], sems[6:8]
    )
    norm_start()
    both_start()
    occ_start()
    norm_wait()
    totals = jnp.sum(all_norms[...], axis=0)
    total_row[...] = totals
    lane = lax.broadcasted_iota(jnp.int32, totals.shape, 1)
    wide = stacked.shape[2] // nb
    ratio_row = jnp.zeros((1, stacked.shape[2]), jnp.float32)
    place = lax.broadcasted_iota(jnp.int32, ratio_row.shape, 1)
    for band in range(nb):
        ratio = band_value(totals, lane, band) / total_pw / band_value(old_row[...], lane, band)
        ratio_row = jnp.where(place // wide == band, ratio, ratio_row)
    for part in range(parts):
        rows = slice(part * owners, (part + 1) * owners)
        moved[:, part, :] = smooth[rows, :] + ratio_row * former[rows, :]
    moved_here[me] = moved[me]
    move_start()
    occ_wait()
    both_wait()
    move_wait()


def begin(sizes, stacked, table, norm_row, old_row, occupied):
    owners, groups, _, _ = sizes
    f32 = jnp.float32
    vmem = pl.BlockSpec(memory_space=pltpu.VMEM)
    lanes, width = norm_row.shape[1], stacked.shape[2]
    parts = table.shape[1] // owners
    sems = []
    for size in (owners, owners, owners, groups):
        sems += [pltpu.SemaphoreType.DMA((size,)), pltpu.SemaphoreType.DMA((size,))]
    return pl.pallas_call(
        functools.partial(begin_kernel, sizes),
        out_shape=[
            jax.ShapeDtypeStruct((owners, 2 * parts, width), f32),
            jax.ShapeDtypeStruct((owners, parts, width), f32),
            jax.ShapeDtypeStruct((groups,) + occupied.shape, f32),
            jax.ShapeDtypeStruct((1, lanes), f32),
        ],
        in_specs=[vmem] * 5,
        out_specs=[vmem] * 4,
        scratch_shapes=[
            pltpu.VMEM((owners, 2 * parts, width), f32),
            pltpu.VMEM((owners, parts, width), f32),
            pltpu.VMEM((parts * owners, width), f32),
            pltpu.VMEM((parts * owners, width), f32),
            pltpu.VMEM((owners, 1, lanes), f32),
        ]
        + sems,
        compiler_params=pltpu.CompilerParams(collective_id=0, has_side_effects=True),
    )(stacked, table, norm_row, old_row, occupied)


def finish_kernel(
    sizes,
    outgoing,
    all_occupied,
    direction,
    curvature_row,
    norm_row,
    started,
    changed,
    returned,
    total_row,
    density,
    rows,
    sums,
    all_sums,
    local_density,
    strips,
    *sems,
):
    owners, groups, nb, total_pw = sizes
    pairs = groups * 2 * nb * nb
    me, my_group = lax.axis_index("pw"), lax.axis_index("band")
    barrier, greetings = greet((("pw", owners), ("band", groups)))

    rows[...] = jnp.zeros_like(rows)

    @pl.loop(0, groups)
    def _(group):
        real, imag = [], []
        for there in range(nb):
            occ_re = all_occupied[group, there]
            occ_im = all_occupied[group, nb + there]
            for here in range(nb):
                dir_re, dir_im = direction[here], direction[nb + here]
                real.append(jnp.sum(occ_re * dir_re + occ_im * dir_im, axis=0, keepdims=True))
                imag.append(jnp.sum(occ_re * dir_im - occ_im * dir_re, axis=0, keepdims=True))
        height = 2 * nb * nb
        start = pl.multiple_of(group * height, height)
        rows[pl.ds(start, height), :] = jnp.concatenate(real + imag, axis=0)

    lanes = lax.dot_general(
        jnp.ones((8, rows.shape[1]), jnp.float32),
        rows[...],
        (((1,), (1,)), ((), ())),
        precision=lax.Precision.HIGHEST,
        preferred_element_type=jnp.float32,
    )
    sums[...] = lanes[0:1] + curvature_row[...]
    all_sums[me] = sums[...]
    returned[me] = outgoing[me]
    pl.semaphore_wait(barrier, greetings)

    sums_start, sums_wait = sender(
        "pw", owners, lambda peer: sums, lambda mine: all_sums.at[mine], sems[0:2]
    )
    back_start, back_wait = sender(
        "pw",
        owners,
        lambda peer: outgoing.at[peer],
        lambda mine: returned.at[mine],
        sems[2:4],
    )
    dens_start, dens_wait = sender(
        "band",
        groups,
        lambda peer: local_density.at[peer],
        lambda mine: strips.at[mine],
        sems[4:6],
    )
    sums_start()
    back_start()
    sums_wait()
    totals = jnp.sum(all_sums[...], axis=0)
    total_row[...] = totals
    lane = lax.broadcasted_iota(jnp.int32, totals.shape, 1)
    steps = []
    for band in range(nb):
        squares = jnp.where((lane < pairs) & (lax.rem(lane, nb) == band), totals * totals, 0.0)
        own = jnp.where(lane == pairs + band, totals, 0.0)
        curvature = jnp.sum(squares + own, axis=1, keepdims=True) / total_pw
        norm = band_value(norm_row[...], lane, band)
        steps.append(norm / curvature)
    planes, width = started.shape[0], started.shape[1] // groups
    for group in range(groups):
        for plane in range(planes):
            part = slice(group * width, (group + 1) * width)
            value = started[plane, part, :]
            for band in range(nb):
                value = value + steps[band] * changed[plane, band, part, :]
            local_density[group, plane * width : (plane + 1) * width, :] = value * (
                4.0 / total_pw
            )
    strips[my_group] = local_density[my_group]
    dens_start()
    dens_wait()
    density[...] = jnp.sum(strips[...], axis=0)
    back_wait()


def finish(sizes, outgoing, all_occupied, direction, curvature_row, norm_row, started, changed):
    owners, groups, nb, _ = sizes
    planes, grid_len = started.shape[0], started.shape[1]
    f32 = jnp.float32
    height = planes * grid_len // groups
    vmem = pl.BlockSpec(memory_space=pltpu.VMEM)
    lanes = curvature_row.shape[1]
    sems = []
    for size in (owners, owners, groups):
        sems += [pltpu.SemaphoreType.DMA((size,)), pltpu.SemaphoreType.DMA((size,))]
    return pl.pallas_call(
        functools.partial(finish_kernel, sizes),
        out_shape=[
            jax.ShapeDtypeStruct(outgoing.shape, f32),
            jax.ShapeDtypeStruct((1, lanes), f32),
            jax.ShapeDtypeStruct((height, started.shape[2]), f32),
        ],
        in_specs=[vmem] * 7,
        out_specs=[vmem] * 3,
        scratch_shapes=[
            pltpu.VMEM((lanes, grid_len), f32),
            pltpu.VMEM((1, lanes), f32),
            pltpu.VMEM((owners, 1, lanes), f32),
            pltpu.VMEM((groups, height, started.shape[2]), f32),
            pltpu.VMEM((groups, height, started.shape[2]), f32),
        ]
        + sems,
        compiler_params=pltpu.CompilerParams(collective_id=1, has_side_effects=True),
    )(outgoing, all_occupied, direction, curvature_row, norm_row, started, changed)


def on_device(
    occupied_bands,
    iterate,
    residual,
    old_direction,
    preconditioner,
    old_norm,
    eigenvalues,
    band_slot,
    potential,
    column_map,
):
    f32 = jnp.float32
    grid_len = potential.shape[1]
    planes = potential.shape[0]
    owners = grid_len // planes
    nb = iterate.shape[1]
    cols = iterate.shape[2]
    slots = band_slot.shape[0]
    groups = slots // nb
    total_pw = column_map.shape[0] * grid_len
    box = grid_len // 2
    wide = -(-cols // 64) * 64
    spare = wide - cols
    full = np.arange(grid_len)
    inner = np.arange(box) - box // 2
    z_forward = rotation(full, full, grid_len, 1.0)
    z_inverse = rotation(full, full, grid_len, -1.0)
    out_table = rotation(full, inner, grid_len, 1.0)
    in_table = rotation(inner, full, grid_len, -1.0)

    by_owner = column_map.reshape(owners, cols)
    wave_x = signed_index(by_owner // grid_len, grid_len) + box // 2
    wave_y = signed_index(by_owner % grid_len, grid_len) + box // 2
    inside = (wave_x >= 0) & (wave_x < box) & (wave_y >= 0) & (wave_y < box)
    cell = jnp.where(inside, wave_x * box + wave_y, -1)
    cell = jnp.pad(cell, ((0, 0), (0, spare)), constant_values=-1).reshape(-1)
    low_count = min(256, box * box)
    high_count = box * box // low_count
    low_hot = (
        jnp.where(cell < 0, -1, cell % low_count)[:, None]
        == jnp.arange(low_count, dtype=jnp.int32)[None, :]
    ).astype(jnp.bfloat16)
    high_hot = (
        jnp.where(cell < 0, -1, cell // low_count)[None, :]
        == jnp.arange(high_count, dtype=jnp.int32)[:, None]
    )

    my_columns = lax.dynamic_slice_in_dim(column_map, lax.axis_index("pw") * cols, cols)
    squares = wave_squares(my_columns, grid_len)
    kinetic = squares.astype(f32) * (4.0 / (grid_len * grid_len))
    sphere = (squares < grid_len // 4 * (grid_len // 4)).astype(f32)
    occupied = occupied_bands * sphere
    start_wave = iterate * sphere
    masked_residual = residual * sphere
    previous = old_direction * sphere
    weight = preconditioner * sphere
    owner_ids = lax.dynamic_slice_in_dim(band_slot, lax.axis_index("band") * nb, nb)
    band_energy = jnp.sum(
        jnp.where(
            owner_ids[:, None] == jnp.arange(slots, dtype=jnp.int32)[None, :],
            eigenvalues[None, :],
            0.0,
        ),
        axis=1,
    )
    smoothed = weight[None] * masked_residual
    norm_local = jnp.sum(smoothed * masked_residual, axis=(0, 2, 3))

    stacked = jnp.stack([occupied, start_wave, smoothed, previous], axis=1)
    stacked = jnp.pad(stacked, ((0, 0), (0, 0), (0, 0), (0, spare), (0, 0)))
    stacked = stacked.reshape(2, 4, nb * wide, grid_len)
    table = z_forward.reshape(2, 2, owners, planes, grid_len).transpose(1, 3, 0, 2, 4)
    lanes = 128
    sizes = (owners, groups, nb, float(total_pw))
    arrived, moved, all_occupied, norms = begin(
        sizes,
        stacked,
        table.reshape(2, planes * 2 * owners, grid_len),
        jnp.pad(norm_local, (0, lanes - nb)).reshape(1, lanes),
        jnp.pad(old_norm, (0, lanes - nb)).reshape(1, lanes),
        occupied.reshape(2 * nb, cols, grid_len),
    )
    new_norm = norms[0, :nb] / total_pw
    beta_ratio = new_norm / old_norm

    direction = smoothed + beta_ratio[None, :, None, None] * previous

    arrived = arrived.reshape(owners, planes, 2, 2, nb, wide).transpose(3, 2, 1, 4, 0, 5)
    moved = moved.reshape(owners, planes, 2, nb, wide).transpose(2, 1, 3, 0, 4)
    fields = jnp.concatenate([arrived, moved[None]], axis=0)
    fields = fields.reshape(3 * 2 * planes * nb, 1, owners * wide)
    high_part, low_part = halves(fields)
    zero = jnp.zeros((), jnp.bfloat16)
    spread = jnp.stack(
        [
            jnp.where(high_hot[None], high_part, zero),
            jnp.where(high_hot[None], low_part, zero),
        ]
    )
    placed = jnp.einsum("hrgc,cl->hrgl", spread, low_hot, preferred_element_type=f32)
    placed = (placed[0] + placed[1]).reshape(3, 2, planes, nb, box, box)
    grid = jnp.einsum("fqpnab,rqyb->frpnay", placed, out_table, precision=mode)
    grid = jnp.einsum("fqpnay,rqxa->frpnxy", grid, out_table, precision=mode)

    occupied_grid = grid[0]
    start_grid = grid[1]
    direction_grid = grid[2]
    started = jnp.sum(occupied_grid * start_grid, axis=(0, 2))
    changed = jnp.sum(occupied_grid * direction_grid, axis=0)
    weighted = potential[None, :, None] * direction_grid
    volume = float(grid_len**3)
    curvature_local = jnp.sum(weighted * direction_grid, axis=(0, 1, 3, 4)) / volume + jnp.sum(
        (kinetic[None, None] - band_energy[None, :, None, None]) * direction * direction,
        axis=(0, 2, 3),
    )

    folded = jnp.einsum("qpnxy,rqax->rpnay", weighted, in_table, precision=mode)
    folded = jnp.einsum("qpnay,rqby->rpnab", folded, in_table, precision=mode)
    folded = folded.reshape(2 * planes * nb, high_count, low_count)
    both = jnp.stack(halves(folded))
    picked = jnp.einsum("hrgl,cl->hrgc", both, low_hot, preferred_element_type=f32)
    picked = picked[0] + picked[1]
    picked = jnp.sum(jnp.where(high_hot[None], picked, 0.0), axis=1)
    picked = picked.reshape(2, planes, nb, owners, wide).transpose(3, 1, 0, 2, 4)
    outgoing = picked.reshape(owners, planes * 2, nb * wide)
    pairs = slots * nb
    returned, totals, density = finish(
        sizes,
        outgoing,
        all_occupied,
        direction.reshape(2 * nb, cols, grid_len),
        jnp.pad(curvature_local, (2 * pairs, lanes - 2 * pairs - nb)).reshape(1, lanes),
        jnp.pad(new_norm, (0, lanes - nb)).reshape(1, lanes),
        started,
        changed,
    )
    density = density.reshape(planes, grid_len // groups, grid_len)
    totals = totals.reshape(-1)
    found = totals[: 2 * pairs].reshape(groups, 2, nb, nb)
    curvature = (
        totals[2 * pairs : 2 * pairs + nb] + jnp.sum(found * found, axis=(0, 1, 2))
    ) / total_pw
    step_size = new_norm / curvature

    returned = returned.reshape(grid_len, 2, nb, wide)
    local_potential = (
        jnp.einsum("zqnc,rqkz->rnck", returned, z_inverse, precision=mode)[:, :, :cols] / volume
    )
    mixing = jnp.stack([found, jnp.stack([-found[:, 1], found[:, 0]], axis=1)], axis=1)
    all_occupied = all_occupied.reshape(groups, 2, nb, cols, grid_len)
    projected = jnp.einsum("gqvck,gqrvn->rnck", all_occupied, mixing, precision=mode)
    image = (
        local_potential * sphere
        + (kinetic[None, None] - band_energy[None, :, None, None]) * direction
        + projected
    )
    new_iterate = start_wave + step_size[None, :, None, None] * direction
    new_residual = masked_residual - step_size[None, :, None, None] * image
    return (new_iterate, new_residual, direction, new_norm, density)


def solution(mesh):
    in_specs = (
        P(None, "band", "pw", None),
        P(None, "band", "pw", None),
        P(None, "band", "pw", None),
        P(None, "band", "pw", None),
        P("band", "pw", None),
        P("band"),
        P(),
        P(),
        P("pw", None, None),
        P(),
    )
    out_specs = (
        P(None, "band", "pw", None),
        P(None, "band", "pw", None),
        P(None, "band", "pw", None),
        P("band"),
        P("pw", "band", None),
    )
    return jax.shard_map(
        on_device, mesh=mesh, in_specs=in_specs, out_specs=out_specs, check_vma=False
    )
```

```python
import functools
import math

import jax
import jax.numpy as jnp
import numpy as np
from jax import lax
from jax.experimental import pallas as pl
from jax.experimental.pallas import tpu as pltpu
from jax.sharding import PartitionSpec as P

mode = lax.Precision.HIGH


def rotation(out_index, in_index, grid_len, sign):
    angles = (np.outer(out_index, in_index) % grid_len) * (2.0 * math.pi / grid_len)
    cosine = np.cos(angles)
    sine = np.sin(angles) * sign
    table = np.stack([np.stack([cosine, -sine]), np.stack([sine, cosine])])
    return jnp.asarray(table.astype(np.float32))


def signed_index(values, grid_len):
    return jnp.where(values < grid_len // 2, values, values - grid_len)


def wave_squares(columns, grid_len):
    wave_x = signed_index(columns // grid_len, grid_len)
    wave_y = signed_index(columns % grid_len, grid_len)
    wave_z = signed_index(jnp.arange(grid_len, dtype=jnp.int32), grid_len)
    return (wave_x * wave_x + wave_y * wave_y)[:, None] + (wave_z * wave_z)[None, :]


def halves(values):
    high = lax.reduce_precision(values, 8, 7)
    return high.astype(jnp.bfloat16), (values - high).astype(jnp.bfloat16)


def greet(axes):
    barrier = pltpu.get_barrier_semaphore()
    for axis, size in axes:
        me = lax.axis_index(axis)

        @pl.loop(1, size)
        def _(step, axis=axis, size=size, me=me):
            pl.semaphore_signal(
                barrier,
                inc=1,
                device_id={axis: lax.rem(me + step, size)},
                device_id_type=pl.DeviceIdType.MESH,
            )

    return barrier, sum(size - 1 for _, size in axes)


def sender(axis, size, source, target, sems):
    me = lax.axis_index(axis)

    def copy_of(step):
        peer = lax.rem(me + step, size)
        return pltpu.make_async_remote_copy(
            src_ref=source(peer),
            dst_ref=target(me),
            send_sem=sems[0].at[step],
            recv_sem=sems[1].at[step],
            device_id={axis: peer},
            device_id_type=pl.DeviceIdType.MESH,
        )

    def start():
        half = size // 2
        copy_of(half).start()

        @pl.loop(1, half)
        def _(near):
            copy_of(half - near).start()
            copy_of(half + near).start()

    def wait():
        @pl.loop(1, size)
        def _(step):
            copy_of(step).wait()

    return start, wait


def band_value(row, lane, band):
    return jnp.sum(jnp.where(lane == band, row, 0.0), axis=1, keepdims=True)


def begin_kernel(
    sizes,
    stacked,
    table,
    norm_row,
    old_row,
    occupied,
    fields,
    all_occupied,
    total_row,
    both_here,
    moved_here,
    both,
    moved,
    smooth,
    former,
    all_norms,
    *sems,
):
    owners, groups, nb, total_pw = sizes
    me, my_group = lax.axis_index("pw"), lax.axis_index("band")
    barrier, greetings = greet((("pw", owners), ("band", groups)))
    parts = table.shape[1] // owners

    def mixed(field):
        return sum(
            lax.dot_general(
                table[part],
                stacked[part, field],
                (((1,), (1,)), ((), ())),
                precision=lax.Precision.HIGHEST,
                preferred_element_type=jnp.float32,
            )
            for part in range(2)
        )

    for field in range(2):
        value = mixed(field)
        for part in range(parts):
            both[:, field * parts + part, :] = value[part * owners : (part + 1) * owners]
    smooth[...] = mixed(2)
    former[...] = mixed(3)
    all_norms[me] = norm_row[...]
    both_here[me] = both[me]
    all_occupied[my_group] = occupied[...]
    pl.semaphore_wait(barrier, greetings)

    norm_start, norm_wait = sender(
        "pw", owners, lambda peer: norm_row, lambda mine: all_norms.at[mine], sems[0:2]
    )
    both_start, both_wait = sender(
        "pw", owners, lambda peer: both.at[peer], lambda mine: both_here.at[mine], sems[2:4]
    )
    move_start, move_wait = sender(
        "pw", owners, lambda peer: moved.at[peer], lambda mine: moved_here.at[mine], sems[4:6]
    )
    occ_start, occ_wait = sender(
        "band", groups, lambda peer: occupied, lambda mine: all_occupied.at[mine], sems[6:8]
    )
    norm_start()
    both_start()
    occ_start()
    norm_wait()
    totals = jnp.sum(all_norms[...], axis=0)
    total_row[...] = totals
    lane = lax.broadcasted_iota(jnp.int32, totals.shape, 1)
    wide = stacked.shape[2] // nb
    ratio_row = jnp.zeros((1, stacked.shape[2]), jnp.float32)
    place = lax.broadcasted_iota(jnp.int32, ratio_row.shape, 1)
    for band in range(nb):
        ratio = band_value(totals, lane, band) / total_pw / band_value(old_row[...], lane, band)
        ratio_row = jnp.where(place // wide == band, ratio, ratio_row)
    for part in range(parts):
        rows = slice(part * owners, (part + 1) * owners)
        moved[:, part, :] = smooth[rows, :] + ratio_row * former[rows, :]
    moved_here[me] = moved[me]
    move_start()
    occ_wait()
    both_wait()

    def join(source, height):
        @pl.loop(0, owners // 2)
        def _(pair):
            first, second = source[2 * pair], source[2 * pair + 1]
            spot = pl.ds(pl.multiple_of(pair * 2 * wide, 2 * wide), 2 * wide)
            near = lax.broadcasted_iota(jnp.int32, first.shape, 1) < wide
            rows = slice(height, height + first.shape[0])
            fields[0, rows, spot] = jnp.where(near, first, pltpu.roll(second, wide, 1))
            fields[1, rows, spot] = jnp.where(near, pltpu.roll(first, wide, 1), second)

    join(both_here, 0)
    move_wait()
    join(moved_here, 2 * parts)


def begin(sizes, stacked, table, norm_row, old_row, occupied):
    owners, groups, _, _ = sizes
    f32 = jnp.float32
    vmem = pl.BlockSpec(memory_space=pltpu.VMEM)
    lanes, width = norm_row.shape[1], stacked.shape[2]
    parts = table.shape[1] // owners
    sems = []
    for size in (owners, owners, owners, groups):
        sems += [pltpu.SemaphoreType.DMA((size,)), pltpu.SemaphoreType.DMA((size,))]
    return pl.pallas_call(
        functools.partial(begin_kernel, sizes),
        out_shape=[
            jax.ShapeDtypeStruct((2, 3 * parts, owners * width // 2), f32),
            jax.ShapeDtypeStruct((groups,) + occupied.shape, f32),
            jax.ShapeDtypeStruct((1, lanes), f32),
        ],
        in_specs=[vmem] * 5,
        out_specs=[vmem] * 3,
        scratch_shapes=[
            pltpu.VMEM((owners, 2 * parts, width), f32),
            pltpu.VMEM((owners, parts, width), f32),
            pltpu.VMEM((owners, 2 * parts, width), f32),
            pltpu.VMEM((owners, parts, width), f32),
            pltpu.VMEM((parts * owners, width), f32),
            pltpu.VMEM((parts * owners, width), f32),
            pltpu.VMEM((owners, 1, lanes), f32),
        ]
        + sems,
        compiler_params=pltpu.CompilerParams(collective_id=0, has_side_effects=True),
    )(stacked, table, norm_row, old_row, occupied)


def finish_kernel(
    sizes,
    outgoing,
    all_occupied,
    direction,
    curvature_row,
    norm_row,
    started,
    changed,
    returned,
    total_row,
    density,
    rows,
    sums,
    all_sums,
    local_density,
    strips,
    *sems,
):
    owners, groups, nb, total_pw = sizes
    pairs = groups * 2 * nb * nb
    me, my_group = lax.axis_index("pw"), lax.axis_index("band")
    barrier, greetings = greet((("pw", owners), ("band", groups)))

    rows[...] = jnp.zeros_like(rows)

    @pl.loop(0, groups)
    def _(group):
        real, imag = [], []
        for there in range(nb):
            occ_re = all_occupied[group, there]
            occ_im = all_occupied[group, nb + there]
            for here in range(nb):
                dir_re, dir_im = direction[here], direction[nb + here]
                real.append(jnp.sum(occ_re * dir_re + occ_im * dir_im, axis=0, keepdims=True))
                imag.append(jnp.sum(occ_re * dir_im - occ_im * dir_re, axis=0, keepdims=True))
        height = 2 * nb * nb
        start = pl.multiple_of(group * height, height)
        rows[pl.ds(start, height), :] = jnp.concatenate(real + imag, axis=0)

    lanes = lax.dot_general(
        jnp.ones((8, rows.shape[1]), jnp.float32),
        rows[...],
        (((1,), (1,)), ((), ())),
        precision=lax.Precision.HIGHEST,
        preferred_element_type=jnp.float32,
    )
    sums[...] = lanes[0:1] + curvature_row[...]
    all_sums[me] = sums[...]
    returned[me] = outgoing[me]
    pl.semaphore_wait(barrier, greetings)

    sums_start, sums_wait = sender(
        "pw", owners, lambda peer: sums, lambda mine: all_sums.at[mine], sems[0:2]
    )
    back_start, back_wait = sender(
        "pw",
        owners,
        lambda peer: outgoing.at[peer],
        lambda mine: returned.at[mine],
        sems[2:4],
    )
    dens_start, dens_wait = sender(
        "band",
        groups,
        lambda peer: local_density.at[peer],
        lambda mine: strips.at[mine],
        sems[4:6],
    )
    sums_start()
    back_start()
    sums_wait()
    totals = jnp.sum(all_sums[...], axis=0)
    total_row[...] = totals
    lane = lax.broadcasted_iota(jnp.int32, totals.shape, 1)
    steps = []
    for band in range(nb):
        squares = jnp.where((lane < pairs) & (lax.rem(lane, nb) == band), totals * totals, 0.0)
        own = jnp.where(lane == pairs + band, totals, 0.0)
        curvature = jnp.sum(squares + own, axis=1, keepdims=True) / total_pw
        norm = band_value(norm_row[...], lane, band) / total_pw
        steps.append(norm / curvature)
    planes, width = started.shape[0], started.shape[1] // groups
    for group in range(groups):
        for plane in range(planes):
            part = slice(group * width, (group + 1) * width)
            value = started[plane, part, :]
            for band in range(nb):
                value = value + steps[band] * changed[plane, band, part, :]
            local_density[group, plane * width : (plane + 1) * width, :] = value * (
                4.0 / total_pw
            )
    strips[my_group] = local_density[my_group]
    dens_start()
    dens_wait()
    density[...] = jnp.sum(strips[...], axis=0)
    back_wait()


def finish(sizes, outgoing, all_occupied, direction, curvature_row, norm_row, started, changed):
    owners, groups, nb, _ = sizes
    planes, grid_len = started.shape[0], started.shape[1]
    f32 = jnp.float32
    height = planes * grid_len // groups
    vmem = pl.BlockSpec(memory_space=pltpu.VMEM)
    lanes = curvature_row.shape[1]
    sems = []
    for size in (owners, owners, groups):
        sems += [pltpu.SemaphoreType.DMA((size,)), pltpu.SemaphoreType.DMA((size,))]
    return pl.pallas_call(
        functools.partial(finish_kernel, sizes),
        out_shape=[
            jax.ShapeDtypeStruct(outgoing.shape, f32),
            jax.ShapeDtypeStruct((1, lanes), f32),
            jax.ShapeDtypeStruct((height, started.shape[2]), f32),
        ],
        in_specs=[vmem] * 7,
        out_specs=[vmem] * 3,
        scratch_shapes=[
            pltpu.VMEM((lanes, grid_len), f32),
            pltpu.VMEM((1, lanes), f32),
            pltpu.VMEM((owners, 1, lanes), f32),
            pltpu.VMEM((groups, height, started.shape[2]), f32),
            pltpu.VMEM((groups, height, started.shape[2]), f32),
        ]
        + sems,
        compiler_params=pltpu.CompilerParams(collective_id=1, has_side_effects=True),
    )(outgoing, all_occupied, direction, curvature_row, norm_row, started, changed)


def on_device(
    occupied_bands,
    iterate,
    residual,
    old_direction,
    preconditioner,
    old_norm,
    eigenvalues,
    band_slot,
    potential,
    column_map,
):
    f32 = jnp.float32
    grid_len = potential.shape[1]
    planes = potential.shape[0]
    owners = grid_len // planes
    nb = iterate.shape[1]
    cols = iterate.shape[2]
    slots = band_slot.shape[0]
    groups = slots // nb
    total_pw = column_map.shape[0] * grid_len
    box = grid_len // 2
    wide = -(-cols // 64) * 64
    spare = wide - cols
    full = np.arange(grid_len)
    inner = np.arange(box) - box // 2
    z_forward = rotation(full, full, grid_len, 1.0)
    z_inverse = rotation(full, full, grid_len, -1.0)
    out_table = rotation(full, inner, grid_len, 1.0)
    in_table = rotation(inner, full, grid_len, -1.0)

    by_owner = column_map.reshape(owners, cols)
    wave_x = signed_index(by_owner // grid_len, grid_len) + box // 2
    wave_y = signed_index(by_owner % grid_len, grid_len) + box // 2
    inside = (wave_x >= 0) & (wave_x < box) & (wave_y >= 0) & (wave_y < box)
    cell = jnp.where(inside, wave_x * box + wave_y, -1)
    cell = jnp.pad(cell, ((0, 0), (0, spare)), constant_values=-1).reshape(-1)
    low_count = min(256, box * box)
    high_count = box * box // low_count
    low_hot = (
        jnp.where(cell < 0, -1, cell % low_count)[:, None]
        == jnp.arange(low_count, dtype=jnp.int32)[None, :]
    ).astype(jnp.bfloat16)
    high_hot = (
        jnp.where(cell < 0, -1, cell // low_count)[None, :]
        == jnp.arange(high_count, dtype=jnp.int32)[:, None]
    )

    my_columns = lax.dynamic_slice_in_dim(column_map, lax.axis_index("pw") * cols, cols)
    squares = wave_squares(my_columns, grid_len)
    kinetic = squares.astype(f32) * (4.0 / (grid_len * grid_len))
    sphere = (squares < grid_len // 4 * (grid_len // 4)).astype(f32)
    occupied = occupied_bands * sphere
    start_wave = iterate * sphere
    masked_residual = residual * sphere
    previous = old_direction * sphere
    weight = preconditioner * sphere
    owner_ids = lax.dynamic_slice_in_dim(band_slot, lax.axis_index("band") * nb, nb)
    band_energy = jnp.sum(
        jnp.where(
            owner_ids[:, None] == jnp.arange(slots, dtype=jnp.int32)[None, :],
            eigenvalues[None, :],
            0.0,
        ),
        axis=1,
    )
    smoothed = weight[None] * masked_residual
    norm_local = jnp.sum(smoothed * masked_residual, axis=(0, 2, 3))

    stacked = jnp.stack([occupied, start_wave, smoothed, previous], axis=1)
    stacked = jnp.pad(stacked, ((0, 0), (0, 0), (0, 0), (0, spare), (0, 0)))
    assert nb == 2 and nb * wide == 128
    stacked = stacked.reshape(2, 4, nb * wide, grid_len)
    table = z_forward.reshape(2, 2, owners, planes, grid_len).transpose(1, 3, 0, 2, 4)
    lanes = 128
    sizes = (owners, groups, nb, float(total_pw))
    fields, all_occupied, norms = begin(
        sizes,
        stacked,
        table.reshape(2, planes * 2 * owners, grid_len),
        jnp.pad(norm_local, (0, lanes - nb)).reshape(1, lanes),
        jnp.pad(old_norm, (0, lanes - nb)).reshape(1, lanes),
        occupied.reshape(2 * nb, cols, grid_len),
    )
    new_norm = norms[0, :nb] / total_pw
    beta_ratio = new_norm / old_norm

    direction = smoothed + beta_ratio[None, :, None, None] * previous

    fields = fields.reshape(3 * 2 * planes * nb, 1, owners * wide)
    high_part, low_part = halves(fields)
    zero = jnp.zeros((), jnp.bfloat16)
    spread = jnp.stack(
        [
            jnp.where(high_hot[None], high_part, zero),
            jnp.where(high_hot[None], low_part, zero),
        ]
    )
    placed = jnp.einsum("hrgc,cl->hrgl", spread, low_hot, preferred_element_type=f32)
    placed = (placed[0] + placed[1]).reshape(nb, 3, planes, 2, box, box)
    grid = jnp.einsum("nfpqab,rqyb->frpnay", placed, out_table, precision=mode)
    grid = jnp.einsum("fqpnay,rqxa->frpnxy", grid, out_table, precision=mode)

    occupied_grid = grid[0]
    start_grid = grid[1]
    direction_grid = grid[2]
    started = jnp.sum(occupied_grid * start_grid, axis=(0, 2))
    changed = jnp.sum(occupied_grid * direction_grid, axis=0)
    weighted = potential[None, :, None] * direction_grid
    volume = float(grid_len**3)
    curvature_local = jnp.sum(weighted * direction_grid, axis=(0, 1, 3, 4)) / volume + jnp.sum(
        (kinetic[None, None] - band_energy[None, :, None, None]) * direction * direction,
        axis=(0, 2, 3),
    )

    folded = jnp.einsum("qpnxy,rqax->rpnay", weighted, in_table, precision=mode)
    folded = jnp.einsum("qpnay,rqby->rpnab", folded, in_table, precision=mode)
    folded = folded.reshape(2 * planes * nb, high_count, low_count)
    both = jnp.stack(halves(folded))
    picked = jnp.einsum("hrgl,cl->hrgc", both, low_hot, preferred_element_type=f32)
    picked = picked[0] + picked[1]
    picked = jnp.sum(jnp.where(high_hot[None], picked, 0.0), axis=1)
    picked = picked.reshape(2, planes, nb, owners, wide).transpose(3, 1, 0, 2, 4)
    outgoing = picked.reshape(owners, planes * 2, nb * wide)
    pairs = slots * nb
    returned, totals, density = finish(
        sizes,
        outgoing,
        all_occupied,
        direction.reshape(2 * nb, cols, grid_len),
        jnp.pad(curvature_local, (2 * pairs, lanes - 2 * pairs - nb)).reshape(1, lanes),
        norms,
        started,
        changed,
    )
    density = density.reshape(planes, grid_len // groups, grid_len)
    totals = totals.reshape(-1)
    found = totals[: 2 * pairs].reshape(groups, 2, nb, nb)
    curvature = (
        totals[2 * pairs : 2 * pairs + nb] + jnp.sum(found * found, axis=(0, 1, 2))
    ) / total_pw
    step_size = new_norm / curvature

    returned = returned.reshape(grid_len, 2, nb, wide)
    local_potential = (
        jnp.einsum("zqnc,rqkz->rnck", returned, z_inverse, precision=mode)[:, :, :cols] / volume
    )
    mixing = jnp.stack([found, jnp.stack([-found[:, 1], found[:, 0]], axis=1)], axis=1)
    all_occupied = all_occupied.reshape(groups, 2, nb, cols, grid_len)
    projected = jnp.einsum("gqvck,gqrvn->rnck", all_occupied, mixing, precision=mode)
    image = (
        local_potential * sphere
        + (kinetic[None, None] - band_energy[None, :, None, None]) * direction
        + projected
    )
    new_iterate = start_wave + step_size[None, :, None, None] * direction
    new_residual = masked_residual - step_size[None, :, None, None] * image
    return (new_iterate, new_residual, direction, new_norm, density)


def solution(mesh):
    in_specs = (
        P(None, "band", "pw", None),
        P(None, "band", "pw", None),
        P(None, "band", "pw", None),
        P(None, "band", "pw", None),
        P("band", "pw", None),
        P("band"),
        P(),
        P(),
        P("pw", None, None),
        P(),
    )
    out_specs = (
        P(None, "band", "pw", None),
        P(None, "band", "pw", None),
        P(None, "band", "pw", None),
        P("band"),
        P("pw", "band", None),
    )
    return jax.shard_map(
        on_device, mesh=mesh, in_specs=in_specs, out_specs=out_specs, check_vma=False
    )
```

```python
import functools
import math

import jax
import jax.numpy as jnp
import numpy as np
from jax import lax
from jax.experimental import pallas as pl
from jax.experimental.pallas import tpu as pltpu
from jax.sharding import PartitionSpec as P

mode = lax.Precision.HIGH


def rotation(out_index, in_index, grid_len, sign):
    angles = (np.outer(out_index, in_index) % grid_len) * (2.0 * math.pi / grid_len)
    cosine = np.cos(angles)
    sine = np.sin(angles) * sign
    table = np.stack([np.stack([cosine, -sine]), np.stack([sine, cosine])])
    return jnp.asarray(table.astype(np.float32))


def signed_index(values, grid_len):
    return jnp.where(values < grid_len // 2, values, values - grid_len)


def wave_squares(columns, grid_len):
    wave_x = signed_index(columns // grid_len, grid_len)
    wave_y = signed_index(columns % grid_len, grid_len)
    wave_z = signed_index(jnp.arange(grid_len, dtype=jnp.int32), grid_len)
    return (wave_x * wave_x + wave_y * wave_y)[:, None] + (wave_z * wave_z)[None, :]


def halves(values):
    high = lax.reduce_precision(values, 8, 7)
    return high.astype(jnp.bfloat16), (values - high).astype(jnp.bfloat16)


def greet(axes):
    barrier = pltpu.get_barrier_semaphore()
    for axis, size in axes:
        me = lax.axis_index(axis)

        @pl.loop(1, size)
        def _(step, axis=axis, size=size, me=me):
            pl.semaphore_signal(
                barrier,
                inc=1,
                device_id={axis: lax.rem(me + step, size)},
                device_id_type=pl.DeviceIdType.MESH,
            )

    return barrier, sum(size - 1 for _, size in axes)


def sender(axis, size, source, target, sems):
    me = lax.axis_index(axis)

    def copy_of(step):
        peer = lax.rem(me + step, size)
        return pltpu.make_async_remote_copy(
            src_ref=source(peer),
            dst_ref=target(me),
            send_sem=sems[0].at[step],
            recv_sem=sems[1].at[step],
            device_id={axis: peer},
            device_id_type=pl.DeviceIdType.MESH,
        )

    def start():
        half = size // 2
        copy_of(half).start()

        @pl.loop(1, half)
        def _(near):
            copy_of(half - near).start()
            copy_of(half + near).start()

    def wait():
        @pl.loop(1, size)
        def _(step):
            copy_of(step).wait()

    return start, wait


def band_value(row, lane, band):
    return jnp.sum(jnp.where(lane == band, row, 0.0), axis=1, keepdims=True)


def begin_kernel(
    sizes,
    stacked,
    table,
    norm_row,
    old_row,
    occupied,
    fields,
    all_occupied,
    total_row,
    both_here,
    moved_here,
    both,
    moved,
    smooth,
    former,
    all_norms,
    *sems,
):
    owners, groups, nb, total_pw = sizes
    me, my_group = lax.axis_index("pw"), lax.axis_index("band")
    barrier, greetings = greet((("pw", owners), ("band", groups)))
    parts = table.shape[1] // owners

    def mixed(field):
        return sum(
            lax.dot_general(
                table[part],
                stacked[part, field],
                (((1,), (1,)), ((), ())),
                precision=lax.Precision.HIGHEST,
                preferred_element_type=jnp.float32,
            )
            for part in range(2)
        )

    for field in range(2):
        value = mixed(field)
        for part in range(parts):
            both[:, field * parts + part, :] = value[part * owners : (part + 1) * owners]
    all_norms[me] = norm_row[...]
    both_here[me] = both[me]
    all_occupied[my_group] = occupied[...]
    pl.semaphore_wait(barrier, greetings)

    norm_start, norm_wait = sender(
        "pw", owners, lambda peer: norm_row, lambda mine: all_norms.at[mine], sems[0:2]
    )
    both_start, both_wait = sender(
        "pw", owners, lambda peer: both.at[peer], lambda mine: both_here.at[mine], sems[2:4]
    )
    move_start, move_wait = sender(
        "pw", owners, lambda peer: moved.at[peer], lambda mine: moved_here.at[mine], sems[4:6]
    )
    occ_start, occ_wait = sender(
        "band", groups, lambda peer: occupied, lambda mine: all_occupied.at[mine], sems[6:8]
    )
    norm_start()
    both_start()
    occ_start()
    smooth[...] = mixed(2)
    former[...] = mixed(3)
    norm_wait()
    totals = jnp.sum(all_norms[...], axis=0)
    total_row[...] = totals
    lane = lax.broadcasted_iota(jnp.int32, totals.shape, 1)
    wide = stacked.shape[2] // nb
    ratio_row = jnp.zeros((1, stacked.shape[2]), jnp.float32)
    place = lax.broadcasted_iota(jnp.int32, ratio_row.shape, 1)
    for band in range(nb):
        ratio = band_value(totals, lane, band) / total_pw / band_value(old_row[...], lane, band)
        ratio_row = jnp.where(place // wide == band, ratio, ratio_row)
    for part in range(parts):
        rows = slice(part * owners, (part + 1) * owners)
        moved[:, part, :] = smooth[rows, :] + ratio_row * former[rows, :]
    moved_here[me] = moved[me]
    move_start()
    occ_wait()
    both_wait()

    def join(source, height):
        @pl.loop(0, owners // 2)
        def _(pair):
            first, second = source[2 * pair], source[2 * pair + 1]
            spot = pl.ds(pl.multiple_of(pair * 2 * wide, 2 * wide), 2 * wide)
            near = lax.broadcasted_iota(jnp.int32, first.shape, 1) < wide
            rows = slice(height, height + first.shape[0])
            fields[0, rows, spot] = jnp.where(near, first, pltpu.roll(second, wide, 1))
            fields[1, rows, spot] = jnp.where(near, pltpu.roll(first, wide, 1), second)

    join(both_here, 0)
    move_wait()
    join(moved_here, 2 * parts)


def begin(sizes, stacked, table, norm_row, old_row, occupied):
    owners, groups, _, _ = sizes
    f32 = jnp.float32
    vmem = pl.BlockSpec(memory_space=pltpu.VMEM)
    lanes, width = norm_row.shape[1], stacked.shape[2]
    parts = table.shape[1] // owners
    sems = []
    for size in (owners, owners, owners, groups):
        sems += [pltpu.SemaphoreType.DMA((size,)), pltpu.SemaphoreType.DMA((size,))]
    return pl.pallas_call(
        functools.partial(begin_kernel, sizes),
        out_shape=[
            jax.ShapeDtypeStruct((2, 3 * parts, owners * width // 2), f32),
            jax.ShapeDtypeStruct((groups,) + occupied.shape, f32),
            jax.ShapeDtypeStruct((1, lanes), f32),
        ],
        in_specs=[vmem] * 5,
        out_specs=[vmem] * 3,
        scratch_shapes=[
            pltpu.VMEM((owners, 2 * parts, width), f32),
            pltpu.VMEM((owners, parts, width), f32),
            pltpu.VMEM((owners, 2 * parts, width), f32),
            pltpu.VMEM((owners, parts, width), f32),
            pltpu.VMEM((parts * owners, width), f32),
            pltpu.VMEM((parts * owners, width), f32),
            pltpu.VMEM((owners, 1, lanes), f32),
        ]
        + sems,
        compiler_params=pltpu.CompilerParams(collective_id=0, has_side_effects=True),
    )(stacked, table, norm_row, old_row, occupied)


def finish_kernel(
    sizes,
    outgoing,
    all_occupied,
    direction,
    curvature_row,
    norm_row,
    started,
    changed,
    returned,
    total_row,
    density,
    rows,
    sums,
    all_sums,
    local_density,
    strips,
    *sems,
):
    owners, groups, nb, total_pw = sizes
    pairs = groups * 2 * nb * nb
    me, my_group = lax.axis_index("pw"), lax.axis_index("band")
    barrier, greetings = greet((("pw", owners), ("band", groups)))

    rows[...] = jnp.zeros_like(rows)

    @pl.loop(0, groups)
    def _(group):
        real, imag = [], []
        for there in range(nb):
            occ_re = all_occupied[group, there]
            occ_im = all_occupied[group, nb + there]
            for here in range(nb):
                dir_re, dir_im = direction[here], direction[nb + here]
                real.append(jnp.sum(occ_re * dir_re + occ_im * dir_im, axis=0, keepdims=True))
                imag.append(jnp.sum(occ_re * dir_im - occ_im * dir_re, axis=0, keepdims=True))
        height = 2 * nb * nb
        start = pl.multiple_of(group * height, height)
        rows[pl.ds(start, height), :] = jnp.concatenate(real + imag, axis=0)

    lanes = lax.dot_general(
        jnp.ones((8, rows.shape[1]), jnp.float32),
        rows[...],
        (((1,), (1,)), ((), ())),
        precision=lax.Precision.HIGHEST,
        preferred_element_type=jnp.float32,
    )
    sums[...] = lanes[0:1] + curvature_row[...]
    all_sums[me] = sums[...]
    returned[me] = outgoing[me]
    pl.semaphore_wait(barrier, greetings)

    sums_start, sums_wait = sender(
        "pw", owners, lambda peer: sums, lambda mine: all_sums.at[mine], sems[0:2]
    )
    back_start, back_wait = sender(
        "pw",
        owners,
        lambda peer: outgoing.at[peer],
        lambda mine: returned.at[mine],
        sems[2:4],
    )
    dens_start, dens_wait = sender(
        "band",
        groups,
        lambda peer: local_density.at[peer],
        lambda mine: strips.at[mine],
        sems[4:6],
    )
    sums_start()
    back_start()
    sums_wait()
    totals = jnp.sum(all_sums[...], axis=0)
    total_row[...] = totals
    lane = lax.broadcasted_iota(jnp.int32, totals.shape, 1)
    steps = []
    for band in range(nb):
        squares = jnp.where((lane < pairs) & (lax.rem(lane, nb) == band), totals * totals, 0.0)
        own = jnp.where(lane == pairs + band, totals, 0.0)
        curvature = jnp.sum(squares + own, axis=1, keepdims=True) / total_pw
        norm = band_value(norm_row[...], lane, band) / total_pw
        steps.append(norm / curvature)
    planes, width = started.shape[0], started.shape[1] // groups
    for group in range(groups):
        for plane in range(planes):
            part = slice(group * width, (group + 1) * width)
            value = started[plane, part, :]
            for band in range(nb):
                value = value + steps[band] * changed[plane, band, part, :]
            local_density[group, plane * width : (plane + 1) * width, :] = value * (
                4.0 / total_pw
            )
    strips[my_group] = local_density[my_group]
    dens_start()
    dens_wait()
    density[...] = jnp.sum(strips[...], axis=0)
    back_wait()


def finish(sizes, outgoing, all_occupied, direction, curvature_row, norm_row, started, changed):
    owners, groups, nb, _ = sizes
    planes, grid_len = started.shape[0], started.shape[1]
    f32 = jnp.float32
    height = planes * grid_len // groups
    vmem = pl.BlockSpec(memory_space=pltpu.VMEM)
    lanes = curvature_row.shape[1]
    sems = []
    for size in (owners, owners, groups):
        sems += [pltpu.SemaphoreType.DMA((size,)), pltpu.SemaphoreType.DMA((size,))]
    return pl.pallas_call(
        functools.partial(finish_kernel, sizes),
        out_shape=[
            jax.ShapeDtypeStruct(outgoing.shape, f32),
            jax.ShapeDtypeStruct((1, lanes), f32),
            jax.ShapeDtypeStruct((height, started.shape[2]), f32),
        ],
        in_specs=[vmem] * 7,
        out_specs=[vmem] * 3,
        scratch_shapes=[
            pltpu.VMEM((lanes, grid_len), f32),
            pltpu.VMEM((1, lanes), f32),
            pltpu.VMEM((owners, 1, lanes), f32),
            pltpu.VMEM((groups, height, started.shape[2]), f32),
            pltpu.VMEM((groups, height, started.shape[2]), f32),
        ]
        + sems,
        compiler_params=pltpu.CompilerParams(collective_id=1, has_side_effects=True),
    )(outgoing, all_occupied, direction, curvature_row, norm_row, started, changed)


def on_device(
    occupied_bands,
    iterate,
    residual,
    old_direction,
    preconditioner,
    old_norm,
    eigenvalues,
    band_slot,
    potential,
    column_map,
):
    f32 = jnp.float32
    grid_len = potential.shape[1]
    planes = potential.shape[0]
    owners = grid_len // planes
    nb = iterate.shape[1]
    cols = iterate.shape[2]
    slots = band_slot.shape[0]
    groups = slots // nb
    total_pw = column_map.shape[0] * grid_len
    box = grid_len // 2
    wide = -(-cols // 64) * 64
    spare = wide - cols
    full = np.arange(grid_len)
    inner = np.arange(box) - box // 2
    z_forward = rotation(full, full, grid_len, 1.0)
    z_inverse = rotation(full, full, grid_len, -1.0)
    out_table = rotation(full, inner, grid_len, 1.0)
    in_table = rotation(inner, full, grid_len, -1.0)

    by_owner = column_map.reshape(owners, cols)
    wave_x = signed_index(by_owner // grid_len, grid_len) + box // 2
    wave_y = signed_index(by_owner % grid_len, grid_len) + box // 2
    inside = (wave_x >= 0) & (wave_x < box) & (wave_y >= 0) & (wave_y < box)
    cell = jnp.where(inside, wave_x * box + wave_y, -1)
    cell = jnp.pad(cell, ((0, 0), (0, spare)), constant_values=-1).reshape(-1)
    low_count = min(256, box * box)
    high_count = box * box // low_count
    low_hot = (
        jnp.where(cell < 0, -1, cell % low_count)[:, None]
        == jnp.arange(low_count, dtype=jnp.int32)[None, :]
    ).astype(jnp.bfloat16)
    high_hot = (
        jnp.where(cell < 0, -1, cell // low_count)[None, :]
        == jnp.arange(high_count, dtype=jnp.int32)[:, None]
    )

    my_columns = lax.dynamic_slice_in_dim(column_map, lax.axis_index("pw") * cols, cols)
    squares = wave_squares(my_columns, grid_len)
    kinetic = squares.astype(f32) * (4.0 / (grid_len * grid_len))
    sphere = (squares < grid_len // 4 * (grid_len // 4)).astype(f32)
    occupied = occupied_bands * sphere
    start_wave = iterate * sphere
    masked_residual = residual * sphere
    previous = old_direction * sphere
    weight = preconditioner * sphere
    owner_ids = lax.dynamic_slice_in_dim(band_slot, lax.axis_index("band") * nb, nb)
    band_energy = jnp.sum(
        jnp.where(
            owner_ids[:, None] == jnp.arange(slots, dtype=jnp.int32)[None, :],
            eigenvalues[None, :],
            0.0,
        ),
        axis=1,
    )
    smoothed = weight[None] * masked_residual
    norm_local = jnp.sum(smoothed * masked_residual, axis=(0, 2, 3))

    stacked = jnp.stack([occupied, start_wave, smoothed, previous], axis=1)
    stacked = jnp.pad(stacked, ((0, 0), (0, 0), (0, 0), (0, spare), (0, 0)))
    assert nb == 2 and nb * wide == 128
    stacked = stacked.reshape(2, 4, nb * wide, grid_len)
    table = z_forward.reshape(2, 2, owners, planes, grid_len).transpose(1, 3, 0, 2, 4)
    lanes = 128
    sizes = (owners, groups, nb, float(total_pw))
    fields, all_occupied, norms = begin(
        sizes,
        stacked,
        table.reshape(2, planes * 2 * owners, grid_len),
        jnp.pad(norm_local, (0, lanes - nb)).reshape(1, lanes),
        jnp.pad(old_norm, (0, lanes - nb)).reshape(1, lanes),
        occupied.reshape(2 * nb, cols, grid_len),
    )
    new_norm = norms[0, :nb] / total_pw
    beta_ratio = new_norm / old_norm

    direction = smoothed + beta_ratio[None, :, None, None] * previous

    fields = fields.reshape(3 * 2 * planes * nb, 1, owners * wide)
    high_part, low_part = halves(fields)
    zero = jnp.zeros((), jnp.bfloat16)
    spread = jnp.stack(
        [
            jnp.where(high_hot[None], high_part, zero),
            jnp.where(high_hot[None], low_part, zero),
        ]
    )
    placed = jnp.einsum("hrgc,cl->hrgl", spread, low_hot, preferred_element_type=f32)
    placed = (placed[0] + placed[1]).reshape(nb, 3, planes, 2, box, box)
    grid = jnp.einsum("nfpqab,rqyb->frpnay", placed, out_table, precision=mode)
    grid = jnp.einsum("fqpnay,rqxa->frpnxy", grid, out_table, precision=mode)

    occupied_grid = grid[0]
    start_grid = grid[1]
    direction_grid = grid[2]
    started = jnp.sum(occupied_grid * start_grid, axis=(0, 2))
    changed = jnp.sum(occupied_grid * direction_grid, axis=0)
    weighted = potential[None, :, None] * direction_grid
    volume = float(grid_len**3)
    curvature_local = jnp.sum(weighted * direction_grid, axis=(0, 1, 3, 4)) / volume + jnp.sum(
        (kinetic[None, None] - band_energy[None, :, None, None]) * direction * direction,
        axis=(0, 2, 3),
    )

    folded = jnp.einsum("qpnxy,rqax->rpnay", weighted, in_table, precision=mode)
    folded = jnp.einsum("qpnay,rqby->rpnab", folded, in_table, precision=mode)
    folded = folded.reshape(2 * planes * nb, high_count, low_count)
    both = jnp.stack(halves(folded))
    picked = jnp.einsum("hrgl,cl->hrgc", both, low_hot, preferred_element_type=f32)
    picked = picked[0] + picked[1]
    picked = jnp.sum(jnp.where(high_hot[None], picked, 0.0), axis=1)
    picked = picked.reshape(2, planes, nb, owners, wide).transpose(3, 1, 0, 2, 4)
    outgoing = picked.reshape(owners, planes * 2, nb * wide)
    pairs = slots * nb
    returned, totals, density = finish(
        sizes,
        outgoing,
        all_occupied,
        direction.reshape(2 * nb, cols, grid_len),
        jnp.pad(curvature_local, (2 * pairs, lanes - 2 * pairs - nb)).reshape(1, lanes),
        norms,
        started,
        changed,
    )
    density = density.reshape(planes, grid_len // groups, grid_len)
    totals = totals.reshape(-1)
    found = totals[: 2 * pairs].reshape(groups, 2, nb, nb)
    curvature = (
        totals[2 * pairs : 2 * pairs + nb] + jnp.sum(found * found, axis=(0, 1, 2))
    ) / total_pw
    step_size = new_norm / curvature

    returned = returned.reshape(grid_len, 2, nb, wide)
    local_potential = (
        jnp.einsum("zqnc,rqkz->rnck", returned, z_inverse, precision=mode)[:, :, :cols] / volume
    )
    mixing = jnp.stack([found, jnp.stack([-found[:, 1], found[:, 0]], axis=1)], axis=1)
    all_occupied = all_occupied.reshape(groups, 2, nb, cols, grid_len)
    projected = jnp.einsum("gqvck,gqrvn->rnck", all_occupied, mixing, precision=mode)
    image = (
        local_potential * sphere
        + (kinetic[None, None] - band_energy[None, :, None, None]) * direction
        + projected
    )
    new_iterate = start_wave + step_size[None, :, None, None] * direction
    new_residual = masked_residual - step_size[None, :, None, None] * image
    return (new_iterate, new_residual, direction, new_norm, density)


def solution(mesh):
    in_specs = (
        P(None, "band", "pw", None),
        P(None, "band", "pw", None),
        P(None, "band", "pw", None),
        P(None, "band", "pw", None),
        P("band", "pw", None),
        P("band"),
        P(),
        P(),
        P("pw", None, None),
        P(),
    )
    out_specs = (
        P(None, "band", "pw", None),
        P(None, "band", "pw", None),
        P(None, "band", "pw", None),
        P("band"),
        P("pw", "band", None),
    )
    return jax.shard_map(
        on_device, mesh=mesh, in_specs=in_specs, out_specs=out_specs, check_vma=False
    )
```
